512 devices in a mesh: occ: 64 (over x, z), vir: 8 (over y, core).
Axes of the slice: x: 4, y: 4, z: 16, core: 2. Of those that a mesh axis runs over, the one named last changes fastest.
Arguments:
- t2_tiles: float32 [64, 8, 4, 128, 256], P('occ', 'vir'), may hold values from -6 to 6
- cycle_ints: float32 [64, 8, 4, 256, 128], P('occ', 'vir'), may hold values from -0.21875 to 0.21875
- cycle_left: int32 [64, 8, 96], P('occ', 'vir'), may hold values from 0 to 3
- cycle_right: int32 [64, 8, 96], P('occ', 'vir'), may hold values from 0 to 3
- cycle_dest: int32 [64, 8, 96], P('occ', 'vir'), may hold values from 0 to 127, as said below
- lam_ladder: float32 [16384, 4096], P('occ', 'vir'), may hold values from -6 to 6
- ladder_ints: float32 [4096, 1024], P('vir'), may hold values from -0.09375 to 0.09375
- ladder_mask: int32 [128, 32], P('occ', 'vir'), may hold values 0 or 1
- partner_slot: int32 [64, 2], P('occ'), may hold values from 0 to 1, as said below
- denom: float32 [16384, 1024], P('occ', 'vir'), may hold values from 1 to 8
Outputs:
- increment: float32 [16384, 1024], P('occ', 'vir')
The draws below stay inside these ranges and needn't reach their ends.
Inputs may be any that keep to these rules, and one draw needn't show every extreme that they name: One device's tasks name each owner (cycle_dest // 2) at most 3 times; in each vir column one owner is named exactly 3 times by every device. `partner_slot`: each row is a permutation of the 2 slots.
All inputs are finite; a program needn't handle non-finite values. No bound on the sum of `ladder_mask` on one device may be relied on, other than what follows from the above.
Results may differ from the reference program's by a relative error of at most 0.0001.
Values sent between devices are 32-bit elements; how exact they have to be, the bound alone decides.
No kernel may reach another device: no remote copies, remote signals or barrier semaphores. Data moves between devices by JAX's collectives and lax.ppermute only.
A program may use at most 128 MiB of HBM per device.

```python
import math
import jax
import jax.numpy as jnp
from jax import lax

TILE = 128
OWN = 2
XT = 4
KC = 256
LB = 4
CAP = 3
TASKS = 96
N_OCC = 64
N_VIR = 8


def draw_cycle_dest(key, part):
    key_hot = jax.random.fold_in(key, 11)
    key_dev = jax.random.fold_in(key, 12)
    key_slot = jax.random.fold_in(key, 13)
    hot = jax.random.randint(key_hot, (N_VIR,), 0, N_OCC)
    hot_rep = jnp.tile(hot, N_OCC)
    keys = jax.random.split(key_dev, N_OCC * N_VIR)

    def single(device_key, hot_owner):
        key_pick, key_order = jax.random.split(device_key)
        others = jnp.arange((N_OCC - 1) * CAP, dtype=jnp.int32) // CAP
        others = others + (others >= hot_owner).astype(jnp.int32)
        picked = jax.random.permutation(key_pick, others)[:TASKS - CAP]
        owners = jnp.concatenate([jnp.full((CAP,), hot_owner, jnp.int32), picked])
        return jax.random.permutation(key_order, owners)
    owners = jax.vmap(single)(keys, hot_rep).reshape(N_OCC, N_VIR, TASKS)
    slots = jax.random.randint(key_slot, (N_OCC, N_VIR, TASKS), 0, OWN)
    return (owners * OWN + slots).astype(jnp.int32)


def draw_partner_slot(key, part):
    keys = jax.random.split(jax.random.fold_in(key, 21), N_OCC)

    def single(row_key):
        return jax.random.permutation(row_key, jnp.arange(OWN, dtype=jnp.int32))
    return jax.vmap(single)(keys).astype(jnp.int32)


def touch_ends(result, rng, least, high):
    longest = result.shape.index(max(result.shape))
    spots = []
    for shift in (0, 1):
        where = [jax.random.randint(jax.random.fold_in(rng, axis), (), 0, length) for axis, length in enumerate(result.shape)]
        where[longest] = (where[longest] + shift) % result.shape[longest]
        spots.append(tuple(where))
    return result.at[spots[0]].set(least).at[spots[1]].set(high)


def block_scale(rng, extent, shards, smallest, top_value):
    level = 1.0
    for position, blocks in shards:
        draws = jax.random.uniform(jax.random.fold_in(jax.random.fold_in(rng, 6), position), (blocks,), jnp.float32, smallest / len(shards), top_value / len(shards))
        level = level * jnp.repeat(jnp.exp(draws), extent[position] // blocks).reshape((-1,) + (1,) * (len(extent) - 1 - position))
    return level


def centred(key, extent, scale, limit, pieces=(), kind=jnp.bfloat16):
    drawn = jax.random.normal(key, extent, jnp.float32) * scale
    if len(pieces) > 0:
        drawn = block_scale(key, extent, pieces, -0.22, 0.18) * drawn
    return jnp.clip(drawn, min=-limit, max=limit).astype(kind)


def setup_inputs(seed: int = 0) -> dict:
    key_of = jax.random.split(jax.random.key(seed), 11)
    t2_tiles = centred(key_of[0], (N_OCC, N_VIR, XT, TILE, KC), 1.0, 6.0, ((0, 64), (1, 8)), jnp.float32)
    cycle_ints = centred(key_of[1], (N_OCC, N_VIR, XT, KC, TILE), (KC * CAP) ** -0.5, 0.21875, ((0, 64), (1, 8)), jnp.float32)
    cycle_left = touch_ends(jax.random.randint(key_of[2], (N_OCC, N_VIR, TASKS), 0, XT), jax.random.fold_in(key_of[2], 1), 0, XT - 1).astype(jnp.int32)
    cycle_right = touch_ends(jax.random.randint(key_of[3], (N_OCC, N_VIR, TASKS), 0, XT), jax.random.fold_in(key_of[3], 1), 0, XT - 1).astype(jnp.int32)
    cycle_dest = draw_cycle_dest(jax.random.fold_in(key_of[10], 71), 0)
    lam_ladder = centred(key_of[5], (N_OCC * OWN * TILE, N_VIR * LB * TILE), 1.0, 6.0, ((0, 64), (1, 8)), jnp.float32)
    ladder_ints = centred(key_of[6], (N_VIR * LB * TILE, N_VIR * TILE), (N_VIR * LB * TILE) ** -0.5, 0.09375, ((0, 8),), jnp.float32)
    ladder_mask = touch_ends((jax.random.randint(key_of[7], (N_OCC * OWN, N_VIR * LB), 0, 4) < 3).astype(jnp.int32), jax.random.fold_in(key_of[7], 1), 0, 1)
    partner_slot = draw_partner_slot(jax.random.fold_in(key_of[10], 71), 0)
    denom = jnp.clip(jnp.exp(math.log(8.0) - 2.0794415 * jax.random.uniform(key_of[9], (N_OCC * OWN * TILE, N_VIR * TILE), jnp.float32) ** block_scale(key_of[9], (N_OCC * OWN * TILE, N_VIR * TILE), ((0, 64), (1, 8)), -0.2, 0.2)), 1.0, 8.0)
    return {"t2_tiles": t2_tiles, "cycle_ints": cycle_ints, "cycle_left": cycle_left, "cycle_right": cycle_right, "cycle_dest": cycle_dest, "lam_ladder": lam_ladder, "ladder_ints": ladder_ints, "ladder_mask": ladder_mask, "partner_slot": partner_slot, "denom": denom}


def reference(t2_tiles, cycle_ints, cycle_left, cycle_right, cycle_dest, lam_ladder, ladder_ints, ladder_mask, partner_slot, denom):
    hi = lax.Precision.HIGHEST
    shaped = lam_ladder.reshape(N_OCC * OWN, TILE, N_VIR * LB, TILE)
    masked = (shaped * ladder_mask.astype(lam_ladder.dtype)[:, None, :, None]).reshape(N_OCC * OWN * TILE, N_VIR * LB * TILE)
    ladder = jnp.dot(masked, ladder_ints, precision=hi)

    def column(q):
        def step(acc, p):
            xs = t2_tiles[p, q]
            ys = cycle_ints[p, q]
            part = jnp.einsum("btk,bkc->btc", xs[cycle_left[p, q]], ys[cycle_right[p, q]], precision=hi)
            return acc + jax.ops.segment_sum(part, cycle_dest[p, q], num_segments=N_OCC * OWN), None
        start = jnp.zeros((N_OCC * OWN, TILE, TILE), t2_tiles.dtype)
        return lax.scan(step, start, jnp.arange(N_OCC, dtype=jnp.int32))[0]

    cycle = lax.map(column, jnp.arange(N_VIR, dtype=jnp.int32))
    cycle = cycle.transpose(1, 2, 0, 3).reshape(N_OCC * OWN * TILE, N_VIR * TILE)
    resid = (ladder + cycle).reshape(N_OCC, OWN, TILE, N_VIR, TILE)
    flipped = resid[::-1]
    partner = jnp.take_along_axis(flipped, partner_slot[:, :, None, None, None], axis=1)
    partner = partner[:, :, ::-1, :, ::-1]
    sym = (resid + partner).reshape(N_OCC * OWN * TILE, N_VIR * TILE)
    return sym / denom
```

```python
import jax
import jax.numpy as jnp
from jax import lax
from jax.experimental import pallas as pl
from jax.experimental.pallas import tpu as pltpu
from jax.sharding import Mesh
from jax.sharding import PartitionSpec as P

CAP = 3
EDGE = 128
OWN = 2
XT = 4
NX = 4
NZ = 16
TASKS = 96
ENTRIES = NX * NZ * CAP
PAIRS = XT * XT
TABLE = 8
ROWS = PAIRS * EDGE + TABLE
NEAR = (0, 1, -1, 2)
HIGHEST = lax.Precision.HIGHEST
SMEM = pltpu.SMEM
VMEM = pltpu.VMEM


def products_kernel(lefts, rights, dests, t2_ref, ints_ref, out_ref, count):
    n_owner = NX * NZ

    def clear(i, c):
        count[i] = 0
        return c

    lax.fori_loop(0, n_owner, clear, 0)
    where = (
        lax.broadcasted_iota(jnp.int32, (TABLE, EDGE), 0) * EDGE
        + lax.broadcasted_iota(jnp.int32, (TABLE, EDGE), 1)
    )

    def place(t, table):
        dest = dests[t]
        owner = dest // OWN
        rank = count[owner]
        count[owner] = rank + 1
        entry = (dest - owner * OWN) * PAIRS + lefts[t] * XT + rights[t]
        return jnp.where(where == owner * CAP + rank, entry, table)

    table = lax.fori_loop(0, TASKS, place, jnp.full((TABLE, EDGE), -1, jnp.int32))
    out_ref[PAIRS * EDGE :, :] = table.astype(jnp.float32)
    right = jnp.concatenate([ints_ref[r] for r in range(XT)], axis=1)
    for l in range(XT):
        tile = jnp.dot(
            t2_ref[l], right, precision=HIGHEST, preferred_element_type=jnp.float32
        )
        for r in range(XT):
            out_ref[pl.ds((l * XT + r) * EDGE, EDGE), :] = tile[:, r * EDGE : (r + 1) * EDGE]


def ladder_kernel(mask, lam_ref, ints_ref, out_ref):
    blocks = lam_ref.shape[1] // EDGE
    for s in range(OWN):
        rows = [
            lam_ref[pl.ds(s * EDGE, EDGE), pl.ds(b * EDGE, EDGE)]
            * mask[s, b].astype(jnp.float32)
            for b in range(blocks)
        ]
        part = jnp.dot(
            jnp.concatenate(rows, axis=1),
            ints_ref[...],
            precision=HIGHEST,
            preferred_element_type=jnp.float32,
        )
        for q in range(out_ref.shape[0]):
            out_ref[q, pl.ds(s * EDGE, EDGE), :] = part[:, q * EDGE : (q + 1) * EDGE]


def gather_kernel(where, t0, t1, t2, t3, p0, p1, p2, p3, o0, o1, o2, o3):
    base = where[0] * NZ
    z = where[1]
    sign = where[2]
    tables = (t0, t1, t2, t3)
    tiles = (p0, p1, p2, p3)
    for near, out in zip(NEAR, (o0, o1, o2, o3)):

        def dest(a, c, near=near, out=out):
            target = lax.rem(z + sign * (near + 4 * a) + 4 * NZ, NZ)
            start = (base + target) * CAP
            acc = [jnp.zeros((EDGE, EDGE), jnp.float32) for _ in range(OWN)]
            for table, tile in zip(tables, tiles):
                for k in range(CAP):
                    entry = table[start + k]
                    slot = lax.shift_right_arithmetic(entry, 4)
                    code = jnp.bitwise_and(jnp.maximum(entry, 0), PAIRS - 1)
                    at = pl.multiple_of(code * EDGE, EDGE)
                    val = tile[pl.ds(at, EDGE), :]
                    for s in range(OWN):
                        acc[s] = acc[s] + val * (slot == s).astype(jnp.float32)
            for s in range(OWN):
                out[a, pl.ds(s * EDGE, EDGE), :] = acc[s]
            return c

        lax.fori_loop(0, 4, dest, 0)


def signed(axis_size, distance):
    pairs = []
    for i in range(axis_size):
        for c in range(2):
            step = distance if c == 0 else -distance
            pairs.append((i * 2 + c, (i + step) % axis_size * 2 + c))
    return pairs


def move(array, axis, size, distance):
    return lax.ppermute(array, (axis, "c"), signed(size, distance))


def vm(n):
    return [pl.BlockSpec(memory_space=VMEM)] * n


def sm(n):
    return [pl.BlockSpec(memory_space=SMEM)] * n


def body(
    t2_tiles,
    cycle_ints,
    cycle_left,
    cycle_right,
    cycle_dest,
    lam_ladder,
    ladder_ints,
    ladder_mask,
    partner_slot,
    denom,
):
    f32 = jnp.float32
    x = lax.axis_index("x")
    z = lax.axis_index("z")
    c = lax.axis_index("c")
    payload = pl.pallas_call(
        products_kernel,
        out_shape=jax.ShapeDtypeStruct((ROWS, EDGE), f32),
        in_specs=sm(3) + vm(2),
        out_specs=pl.BlockSpec(memory_space=VMEM),
        scratch_shapes=[pltpu.SMEM((NX * NZ,), jnp.int32)],
        name="products",
    )(cycle_left[0, 0], cycle_right[0, 0], cycle_dest[0, 0], t2_tiles[0, 0], cycle_ints[0, 0])
    got_a = move(payload, "x", NX, 1)
    got_b = move(payload, "x", NX, -1)
    got_c = move(got_a, "x", NX, 1)
    partial = pl.pallas_call(
        ladder_kernel,
        out_shape=jax.ShapeDtypeStruct((8, OWN * EDGE, EDGE), f32),
        in_specs=sm(1) + vm(2),
        out_specs=pl.BlockSpec(memory_space=VMEM),
        name="ladder",
    )(ladder_mask, lam_ladder, ladder_ints)
    spread = lax.all_to_all(partial, ("y", "c"), split_axis=0, concat_axis=0, tiled=True)
    ladder = jnp.sum(spread, axis=0)

    arrays = (payload, got_a, got_b, got_c)
    tables = [a[PAIRS * EDGE :].reshape(-1)[:ENTRIES].astype(jnp.int32) for a in arrays]
    place = jnp.stack([x, z, 1 - 2 * c]).astype(jnp.int32)
    near = pl.pallas_call(
        gather_kernel,
        out_shape=[jax.ShapeDtypeStruct((4, OWN * EDGE, EDGE), f32)] * 4,
        in_specs=sm(5) + vm(4),
        out_specs=vm(4),
        name="gather",
    )(place, *tables, *arrays)
    moved = [move(near[j], "z", NZ, NEAR[j]) for j in (1, 2, 3)]
    far = [near[0][a] + moved[0][a] + moved[1][a] + moved[2][a] for a in range(4)]
    far = [far[0]] + [move(far[a], "z", NZ, 4 * a) for a in (1, 3, 2)]
    resid = (ladder + far[0] + far[1] + far[2] + far[3]).reshape(OWN, EDGE, EDGE)
    n_occ = NX * NZ
    other = lax.ppermute(resid, ("x", "z"), [(i, n_occ - 1 - i) for i in range(n_occ)])
    partner = other[partner_slot[0]][:, ::-1, ::-1]
    return (resid + partner).reshape(OWN * EDGE, EDGE) / denom


def solution(mesh):
    grid = Mesh(mesh.devices.reshape(NX, NZ, 4, 2), ("x", "z", "y", "c"))
    occ = ("x", "z")
    vir = ("y", "c")
    in_specs = (
        P(occ, vir, None, None, None),
        P(occ, vir, None, None, None),
        P(occ, vir, None),
        P(occ, vir, None),
        P(occ, vir, None),
        P(occ, vir),
        P(vir, None),
        P(occ, vir),
        P(occ, None),
        P(occ, vir),
    )
    return jax.shard_map(
        body, mesh=grid, in_specs=in_specs, out_specs=P(occ, vir), check_vma=False
    )
```

```python
import functools

import jax
import jax.numpy as jnp
from jax import lax
from jax.experimental import pallas as pl
from jax.experimental.pallas import tpu as pltpu
from jax.sharding import Mesh
from jax.sharding import PartitionSpec as P

CAP = 3
EDGE = 128
OWN = 2
XT = 4
NX = 4
NZ = 16
TASKS = 96
ENTRIES = NX * NZ * CAP
PAIRS = XT * XT
TABLE = 8
ROWS = PAIRS * EDGE + TABLE
HIGH = 4
LOW = 4
NEAR = (0, 1, -1, 2)
HIGHEST = lax.Precision.HIGHEST
SMEM = pltpu.SMEM
VMEM = pltpu.VMEM


def products_kernel(lefts, rights, dests, t2_ref, ints_ref, out_ref, count):
    n_owner = NX * NZ

    def clear(i, c):
        count[i] = 0
        return c

    lax.fori_loop(0, n_owner, clear, 0)
    where = (
        lax.broadcasted_iota(jnp.int32, (TABLE, EDGE), 0) * EDGE
        + lax.broadcasted_iota(jnp.int32, (TABLE, EDGE), 1)
    )

    def place(t, table):
        dest = dests[t]
        owner = dest // OWN
        rank = count[owner]
        count[owner] = rank + 1
        entry = (dest - owner * OWN) * PAIRS + lefts[t] * XT + rights[t]
        return jnp.where(where == owner * CAP + rank, entry, table)

    table = lax.fori_loop(0, TASKS, place, jnp.full((TABLE, EDGE), -1, jnp.int32))
    out_ref[PAIRS * EDGE :, :] = table.astype(jnp.float32)
    right = jnp.concatenate([ints_ref[r] for r in range(XT)], axis=1)
    for l in range(XT):
        tile = jnp.dot(
            t2_ref[l], right, precision=HIGHEST, preferred_element_type=jnp.float32
        )
        for r in range(XT):
            out_ref[pl.ds((l * XT + r) * EDGE, EDGE), :] = tile[:, r * EDGE : (r + 1) * EDGE]


def ladder_kernel(mask, lam_ref, ints_ref, out_ref):
    blocks = lam_ref.shape[1] // EDGE
    for s in range(OWN):
        rows = [
            lam_ref[pl.ds(s * EDGE, EDGE), pl.ds(b * EDGE, EDGE)]
            * mask[s, b].astype(jnp.float32)
            for b in range(blocks)
        ]
        part = jnp.dot(
            jnp.concatenate(rows, axis=1),
            ints_ref[...],
            precision=HIGHEST,
            preferred_element_type=jnp.float32,
        )
        for q in range(out_ref.shape[0]):
            out_ref[q, pl.ds(s * EDGE, EDGE), :] = part[:, q * EDGE : (q + 1) * EDGE]


def flipped(value):
    last = value.shape[0] // 8 - 1
    lane = EDGE - 1 - lax.broadcasted_iota(jnp.int32, (8, EDGE), 1)
    row = 7 - lax.broadcasted_iota(jnp.int32, (8, EDGE), 0)
    parts = []
    for i in range(last + 1):
        part = value[(last - i) * 8 : (last - i + 1) * 8]
        part = jnp.take_along_axis(part, lane, axis=1, mode="promise_in_bounds")
        part = jnp.take_along_axis(part, row, axis=0, mode="promise_in_bounds")
        parts.append(part)
    return jnp.concatenate(parts, axis=0)


def gather_kernel(sources, more, place, slots, *refs):
    tables = refs[:sources]
    tiles = refs[sources : 2 * sources]
    refs = refs[2 * sources :]
    befores = refs[:4] if more else (None,) * 4
    outs = refs[-4:]
    base = place[0] * NZ
    z = place[1]
    sign = place[2]
    for near, before, out in zip(NEAR, befores, outs):
        low = jnp.bitwise_and(z + sign * near + NZ, LOW - 1)

        def dest(a, carry, low=low, before=before, out=out):
            target = a * LOW + low
            owner = base + target
            sums = []
            for flip in range(2):
                start = (NX * NZ - 1 - owner if flip else owner) * CAP
                acc = [jnp.zeros((EDGE, EDGE), jnp.float32) for _ in range(OWN)]
                for table, tile in zip(tables, tiles):
                    for k in range(CAP):
                        entry = table[start + k]
                        slot = lax.shift_right_arithmetic(entry, 4)
                        code = jnp.bitwise_and(jnp.maximum(entry, 0), PAIRS - 1)
                        val = tile[pl.ds(pl.multiple_of(code * EDGE, EDGE), EDGE), :]
                        for s in range(OWN):
                            want = slots[target * OWN + s] if flip else s
                            acc[s] = acc[s] + val * (slot == want).astype(jnp.float32)
                sums.append(acc)
            for s in range(OWN):
                rows = pl.ds(s * EDGE, EDGE)
                total = sums[0][s] + flipped(sums[1][s])
                if before is not None:
                    total = total + before[a, rows, :]
                out[a, rows, :] = total
            return carry

        lax.fori_loop(0, HIGH, dest, 0)


def signed(axis_size, distance):
    pairs = []
    for i in range(axis_size):
        for c in range(2):
            step = distance if c == 0 else -distance
            pairs.append((i * 2 + c, (i + step) % axis_size * 2 + c))
    return pairs


def move_x(array, distance):
    return lax.ppermute(array, ("x", "c"), signed(NX, distance))


def move_z(array, distance):
    return lax.ppermute(array, ("h", "l", "c"), signed(NZ, distance))


def gather(place, slots, tables, arrays, before=()):
    n = len(arrays)
    return pl.pallas_call(
        functools.partial(gather_kernel, n, len(before) > 0),
        out_shape=[jax.ShapeDtypeStruct((HIGH, OWN * EDGE, EDGE), jnp.float32)] * 4,
        in_specs=sm(2 + n) + vm(n + len(before)),
        out_specs=vm(4),
        name="gather_more" if before else "gather",
    )(place, slots, *tables, *arrays, *before)


def vm(n):
    return [pl.BlockSpec(memory_space=VMEM)] * n


def sm(n):
    return [pl.BlockSpec(memory_space=SMEM)] * n


def body(
    t2_tiles,
    cycle_ints,
    cycle_left,
    cycle_right,
    cycle_dest,
    lam_ladder,
    ladder_ints,
    ladder_mask,
    partner_slot,
    denom,
):
    f32 = jnp.float32
    x = lax.axis_index("x")
    z = lax.axis_index(("h", "l"))
    c = lax.axis_index("c")
    place = jnp.stack([x, z, 1 - 2 * c]).astype(jnp.int32)
    payload = pl.pallas_call(
        products_kernel,
        out_shape=jax.ShapeDtypeStruct((ROWS, EDGE), f32),
        in_specs=sm(3) + vm(2),
        out_specs=pl.BlockSpec(memory_space=VMEM),
        scratch_shapes=[pltpu.SMEM((NX * NZ,), jnp.int32)],
        name="products",
    )(cycle_left[0, 0], cycle_right[0, 0], cycle_dest[0, 0], t2_tiles[0, 0], cycle_ints[0, 0])
    got_a = move_x(payload, 1)
    got_b = move_x(payload, -1)
    got_c = move_x(got_a, 1)
    partial = pl.pallas_call(
        ladder_kernel,
        out_shape=jax.ShapeDtypeStruct((8, OWN * EDGE, EDGE), f32),
        in_specs=sm(1) + vm(2),
        out_specs=pl.BlockSpec(memory_space=VMEM),
        name="ladder",
    )(ladder_mask, lam_ladder, ladder_ints)
    spread = lax.all_to_all(partial, ("y", "c"), split_axis=0, concat_axis=0, tiled=True)
    ladder = jnp.sum(spread, axis=0)
    n_occ = NX * NZ
    mirror = [(i, n_occ - 1 - i) for i in range(n_occ)]
    other = lax.ppermute(ladder, ("x", "h", "l"), mirror).reshape(OWN, EDGE, EDGE)
    other = other[partner_slot[0]][:, ::-1, ::-1].reshape(OWN * EDGE, EDGE)
    ladder = ladder + other
    own_slots = jnp.broadcast_to(partner_slot, (NZ, OWN))
    slots = lax.all_to_all(own_slots, ("h", "l"), split_axis=0, concat_axis=0, tiled=True)
    slots = slots.reshape(-1)

    arrays = (payload, got_a, got_b, got_c)
    tables = [a[PAIRS * EDGE :].reshape(-1)[:ENTRIES].astype(jnp.int32) for a in arrays]
    near = gather(place, slots, tables[:3], arrays[:3])
    near = gather(place, slots, tables[3:], arrays[3:], near)
    moved = [move_z(near[j], NEAR[j]) for j in (3, 1, 2)]
    far = near[0] + moved[0] + moved[1] + moved[2]
    far = lax.all_to_all(far, "h", split_axis=0, concat_axis=0, tiled=True)
    return (ladder + far[0] + far[1] + far[2] + far[3]) / denom


def solution(mesh):
    grid = Mesh(mesh.devices.reshape(NX, HIGH, LOW, 4, 2), ("x", "h", "l", "y", "c"))
    occ = ("x", "h", "l")
    vir = ("y", "c")
    in_specs = (
        P(occ, vir, None, None, None),
        P(occ, vir, None, None, None),
        P(occ, vir, None),
        P(occ, vir, None),
        P(occ, vir, None),
        P(occ, vir),
        P(vir, None),
        P(occ, vir),
        P(occ, None),
        P(occ, vir),
    )
    return jax.shard_map(
        body, mesh=grid, in_specs=in_specs, out_specs=P(occ, vir), check_vma=False
    )
```

```python
import functools

import jax
import jax.numpy as jnp
from jax import lax
from jax.experimental import pallas as pl
from jax.experimental.pallas import tpu as pltpu
from jax.sharding import Mesh
from jax.sharding import PartitionSpec as P

CAP = 3
EDGE = 128
OWN = 2
XT = 4
NX = 4
NZ = 16
TASKS = 96
ENTRIES = NX * NZ * CAP
PAIRS = XT * XT
TABLE = 8
ROWS = PAIRS * EDGE + TABLE
HIGH = 4
LOW = 4
NEAR = (2, 1, -1, 0)
HIGHEST = lax.Precision.HIGHEST
SMEM = pltpu.SMEM
VMEM = pltpu.VMEM


def halves(value):
    high = value.astype(jnp.bfloat16)
    return high, (value - high.astype(jnp.float32)).astype(jnp.bfloat16)


def dot3(left, right):
    left_high, left_low = halves(left)
    right_high, right_low = halves(right)
    dot = functools.partial(jnp.dot, preferred_element_type=jnp.float32)
    return dot(left_high, right_high) + (dot(left_high, right_low) + dot(left_low, right_high))


def products_kernel(lefts, rights, dests, t2_ref, ints_ref, out_ref, count):
    for i in range(NX * NZ):
        count[i] = 0
    where = (
        lax.broadcasted_iota(jnp.int32, (TABLE, EDGE), 0) * EDGE
        + lax.broadcasted_iota(jnp.int32, (TABLE, EDGE), 1)
    )
    table = jnp.full((TABLE, EDGE), -1, jnp.int32)
    for t in range(TASKS):
        dest = dests[t]
        owner = lax.shift_right_logical(dest, 1)
        rank = count[owner]
        count[owner] = rank + 1
        entry = jnp.bitwise_and(dest, OWN - 1) * PAIRS + lefts[t] * XT + rights[t]
        table = jnp.where(where == owner * CAP + rank, entry, table)
    out_ref[PAIRS * EDGE :, :] = table.astype(jnp.float32)
    right = jnp.concatenate([ints_ref[r] for r in range(XT)], axis=1)
    for l in range(XT):
        tile = dot3(t2_ref[l], right)
        for r in range(XT):
            out_ref[pl.ds((l * XT + r) * EDGE, EDGE), :] = tile[:, r * EDGE : (r + 1) * EDGE]


def ladder_kernel(mask, lam_ref, ints_ref, out_ref):
    blocks = lam_ref.shape[1] // EDGE
    for s in range(OWN):
        rows = [
            lam_ref[pl.ds(s * EDGE, EDGE), pl.ds(b * EDGE, EDGE)]
            * mask[s, b].astype(jnp.float32)
            for b in range(blocks)
        ]
        part = dot3(jnp.concatenate(rows, axis=1), ints_ref[...])
        for q in range(out_ref.shape[0]):
            out_ref[q, pl.ds(s * EDGE, EDGE), :] = part[:, q * EDGE : (q + 1) * EDGE]


def flipped(value):
    last = value.shape[0] // 8 - 1
    lane = EDGE - 1 - lax.broadcasted_iota(jnp.int32, (8, EDGE), 1)
    row = 7 - lax.broadcasted_iota(jnp.int32, (8, EDGE), 0)
    parts = []
    for i in range(last + 1):
        part = value[(last - i) * 8 : (last - i + 1) * 8]
        part = jnp.take_along_axis(part, lane, axis=1, mode="promise_in_bounds")
        part = jnp.take_along_axis(part, row, axis=0, mode="promise_in_bounds")
        parts.append(part)
    return jnp.concatenate(parts, axis=0)


def gather_kernel(sources, nears, more, slots, *refs):
    tiles = refs[:sources]
    refs = refs[sources:]
    befores = refs[: len(nears)] if more else (None,) * len(nears)
    refs = refs[len(nears) :] if more else refs
    outs = refs[: len(nears)]
    tables, sems = refs[len(nears) :]
    copies = [
        pltpu.make_async_copy(tile.at[pl.ds(PAIRS * EDGE, TABLE)], tables.at[i], sems.at[i])
        for i, tile in enumerate(tiles)
    ]
    for copy in copies:
        copy.start()
    base = lax.axis_index("x") * NZ
    z = lax.axis_index("h") * LOW + lax.axis_index("l")
    sign = 1 - 2 * lax.axis_index("c")
    for copy in copies:
        copy.wait()
    for near, before, out in zip(nears, befores, outs):
        low = jnp.bitwise_and(z + sign * near + NZ, LOW - 1)

        def dest(a, carry, low=low, before=before, out=out):
            target = a * LOW + low
            owner = base + target
            sums = []
            for flip in range(2):
                start = (NX * NZ - 1 - owner if flip else owner) * CAP
                acc = [jnp.zeros((EDGE, EDGE), jnp.float32) for _ in range(OWN)]
                for i, tile in enumerate(tiles):
                    for k in range(CAP):
                        at = start + k
                        row = lax.shift_right_logical(at, 7)
                        lane = jnp.bitwise_and(at, EDGE - 1)
                        entry = tables[i, row, lane].astype(jnp.int32)
                        slot = lax.shift_right_arithmetic(entry, 4)
                        code = jnp.bitwise_and(jnp.maximum(entry, 0), PAIRS - 1)
                        val = tile[pl.ds(pl.multiple_of(code * EDGE, EDGE), EDGE), :]
                        for s in range(OWN):
                            want = slots[target, s] if flip else s
                            acc[s] = acc[s] + val * (slot == want).astype(jnp.float32)
                sums.append(acc)
            for s in range(OWN):
                rows = pl.ds(s * EDGE, EDGE)
                total = sums[0][s] + flipped(sums[1][s])
                if before is not None:
                    total = total + before[a, rows, :]
                out[a, rows, :] = total
            return carry

        lax.fori_loop(0, HIGH, dest, 0)


def signed(axis_size, distance):
    pairs = []
    for i in range(axis_size):
        for c in range(2):
            step = distance if c == 0 else -distance
            pairs.append((i * 2 + c, (i + step) % axis_size * 2 + c))
    return pairs


def move_x(array, distance):
    return lax.ppermute(array, ("x", "c"), signed(NX, distance))


def move_z(array, distance):
    return lax.ppermute(array, ("h", "l", "c"), signed(NZ, distance))


def gather(nears, slots, arrays, before=()):
    n = len(arrays)
    return pl.pallas_call(
        functools.partial(gather_kernel, n, nears, len(before) > 0),
        out_shape=[jax.ShapeDtypeStruct((HIGH, OWN * EDGE, EDGE), jnp.float32)] * len(nears),
        in_specs=sm(1) + vm(n + len(before)),
        out_specs=vm(len(nears)),
        scratch_shapes=[pltpu.SMEM((n, TABLE, EDGE), jnp.float32), pltpu.SemaphoreType.DMA((n,))],
        name="gather_more" if before else "gather",
    )(slots, *arrays, *before)


def vm(n):
    return [pl.BlockSpec(memory_space=VMEM)] * n


def sm(n):
    return [pl.BlockSpec(memory_space=SMEM)] * n


def body(
    t2_tiles,
    cycle_ints,
    cycle_left,
    cycle_right,
    cycle_dest,
    lam_ladder,
    ladder_ints,
    ladder_mask,
    partner_slot,
    denom,
):
    f32 = jnp.float32
    payload = pl.pallas_call(
        products_kernel,
        out_shape=jax.ShapeDtypeStruct((ROWS, EDGE), f32),
        in_specs=sm(3) + vm(2),
        out_specs=pl.BlockSpec(memory_space=VMEM),
        scratch_shapes=[pltpu.SMEM((NX * NZ,), jnp.int32)],
        name="products",
    )(cycle_left[0, 0], cycle_right[0, 0], cycle_dest[0, 0], t2_tiles[0, 0], cycle_ints[0, 0])
    got_a = move_x(payload, 1)
    got_b = move_x(payload, -1)
    partial = pl.pallas_call(
        ladder_kernel,
        out_shape=jax.ShapeDtypeStruct((8, OWN * EDGE, EDGE), f32),
        in_specs=sm(1) + vm(2),
        out_specs=pl.BlockSpec(memory_space=VMEM),
        name="ladder",
    )(ladder_mask, lam_ladder, ladder_ints)
    own_slots = jnp.broadcast_to(partner_slot, (NZ, OWN))
    slots = lax.all_to_all(own_slots, ("h", "l"), split_axis=0, concat_axis=0, tiled=True)
    got_a, got_b, slots, partial = lax.optimization_barrier((got_a, got_b, slots, partial))
    got_c = move_x(got_a, 1)

    near = gather(NEAR, slots, (payload, got_a, got_b))
    near, partial = lax.optimization_barrier((near, partial))
    spread = lax.all_to_all(partial, ("y", "c"), split_axis=0, concat_axis=0, tiled=True)
    ladder = jnp.sum(spread, axis=0)
    n_occ = NX * NZ
    mirror = [(i, n_occ - 1 - i) for i in range(n_occ)]
    other = lax.ppermute(ladder, ("x", "h", "l"), mirror)

    first = gather(NEAR[:1], slots, (got_c,), near[:1])
    moved = [move_z(first[0], NEAR[0])]
    first, others = lax.optimization_barrier((first, near[1:]))
    rest = gather(NEAR[1:], slots, (got_c,), others)
    moved += [move_z(rest[j], NEAR[1 + j]) for j in range(2)]
    far = rest[2] + moved[0] + moved[1] + moved[2]
    far, other = lax.optimization_barrier((far, other))
    far = lax.all_to_all(far, "h", split_axis=0, concat_axis=0, tiled=True)
    other = other.reshape(OWN, EDGE, EDGE)[partner_slot[0]][:, ::-1, ::-1]
    ladder = ladder + other.reshape(OWN * EDGE, EDGE)
    return (ladder + far[0] + far[1] + far[2] + far[3]) / denom


def solution(mesh):
    grid = Mesh(mesh.devices.reshape(NX, HIGH, LOW, 4, 2), ("x", "h", "l", "y", "c"))
    occ = ("x", "h", "l")
    vir = ("y", "c")
    in_specs = (
        P(occ, vir, None, None, None),
        P(occ, vir, None, None, None),
        P(occ, vir, None),
        P(occ, vir, None),
        P(occ, vir, None),
        P(occ, vir),
        P(vir, None),
        P(occ, vir),
        P(occ, None),
        P(occ, vir),
    )
    return jax.shard_map(
        body, mesh=grid, in_specs=in_specs, out_specs=P(occ, vir), check_vma=False
    )
```

```python
import functools

import jax
import jax.numpy as jnp
from jax import lax
from jax.experimental import pallas as pl
from jax.experimental.pallas import tpu as pltpu
from jax.sharding import Mesh
from jax.sharding import PartitionSpec as P

CAP = 3
EDGE = 128
OWN = 2
XT = 4
NX = 4
NZ = 16
TASKS = 96
ENTRIES = NX * NZ * CAP
PAIRS = XT * XT
TABLE = 8
ROWS = PAIRS * EDGE + TABLE
HIGH = 4
LOW = 4
NEAR = (2, 1, -1, 0)
HIGHEST = lax.Precision.HIGHEST
SMEM = pltpu.SMEM
VMEM = pltpu.VMEM


def halves(value):
    high = value.astype(jnp.bfloat16)
    return high, (value - high.astype(jnp.float32)).astype(jnp.bfloat16)


def dot3(left, right):
    left_high, left_low = halves(left)
    right_high, right_low = halves(right)
    dot = functools.partial(jnp.dot, preferred_element_type=jnp.float32)
    return dot(left_high, right_high) + (dot(left_high, right_low) + dot(left_low, right_high))


def products_kernel(lefts, rights, dests, t2_ref, ints_ref, out_ref, count):
    for i in range(NX * NZ):
        count[i] = 0
    where = (
        lax.broadcasted_iota(jnp.int32, (TABLE, EDGE), 0) * EDGE
        + lax.broadcasted_iota(jnp.int32, (TABLE, EDGE), 1)
    )
    table = jnp.full((TABLE, EDGE), -1, jnp.int32)
    for t in range(TASKS):
        dest = dests[t]
        owner = lax.shift_right_logical(dest, 1)
        rank = count[owner]
        count[owner] = rank + 1
        entry = jnp.bitwise_and(dest, OWN - 1) * PAIRS + lefts[t] * XT + rights[t]
        table = jnp.where(where == owner * CAP + rank, entry, table)
    out_ref[PAIRS * EDGE :, :] = table.astype(jnp.float32)
    right = jnp.concatenate([ints_ref[r] for r in range(XT)], axis=1)
    for l in range(XT):
        tile = dot3(t2_ref[l], right)
        for r in range(XT):
            out_ref[pl.ds((l * XT + r) * EDGE, EDGE), :] = tile[:, r * EDGE : (r + 1) * EDGE]


def ladder_kernel(mask, lam_ref, ints_ref, out_ref):
    blocks = lam_ref.shape[1] // EDGE
    for s in range(OWN):
        rows = [
            lam_ref[pl.ds(s * EDGE, EDGE), pl.ds(b * EDGE, EDGE)]
            * mask[s, b].astype(jnp.float32)
            for b in range(blocks)
        ]
        part = dot3(jnp.concatenate(rows, axis=1), ints_ref[...])
        for q in range(out_ref.shape[0]):
            out_ref[q, pl.ds(s * EDGE, EDGE), :] = part[:, q * EDGE : (q + 1) * EDGE]


def flipped(value):
    last = value.shape[0] // 8 - 1
    lane = EDGE - 1 - lax.broadcasted_iota(jnp.int32, (8, EDGE), 1)
    row = 7 - lax.broadcasted_iota(jnp.int32, (8, EDGE), 0)
    parts = []
    for i in range(last + 1):
        part = value[(last - i) * 8 : (last - i + 1) * 8]
        part = jnp.take_along_axis(part, lane, axis=1, mode="promise_in_bounds")
        part = jnp.take_along_axis(part, row, axis=0, mode="promise_in_bounds")
        parts.append(part)
    return jnp.concatenate(parts, axis=0)


def gather_kernel(sources, more, slots, *refs):
    tiles = refs[:sources]
    refs = refs[sources:]
    cells = [(near, s) for near in NEAR for s in range(OWN)]
    befores = refs[: len(cells)] if more else (None,) * len(cells)
    refs = refs[len(cells) :] if more else refs
    outs = refs[: len(cells)]
    tables, sems = refs[len(cells) :]
    copies = [
        pltpu.make_async_copy(tile.at[pl.ds(PAIRS * EDGE, TABLE)], tables.at[i], sems.at[i])
        for i, tile in enumerate(tiles)
    ]
    for copy in copies:
        copy.start()
    base = lax.axis_index("x") * NZ
    z = lax.axis_index("h") * LOW + lax.axis_index("l")
    sign = 1 - 2 * lax.axis_index("c")
    for copy in copies:
        copy.wait()
    for j, near in enumerate(NEAR):
        low = jnp.bitwise_and(z + sign * near + NZ, LOW - 1)

        def dest(a, carry, low=low, j=j):
            target = a * LOW + low
            owner = base + target
            sums = []
            for flip in range(2):
                start = (NX * NZ - 1 - owner if flip else owner) * CAP
                acc = [jnp.zeros((EDGE, EDGE), jnp.float32) for _ in range(OWN)]
                for i, tile in enumerate(tiles):
                    for k in range(CAP):
                        at = start + k
                        row = lax.shift_right_logical(at, 7)
                        lane = jnp.bitwise_and(at, EDGE - 1)
                        entry = tables[i, row, lane].astype(jnp.int32)
                        slot = lax.shift_right_arithmetic(entry, 4)
                        code = jnp.bitwise_and(jnp.maximum(entry, 0), PAIRS - 1)
                        val = tile[pl.ds(pl.multiple_of(code * EDGE, EDGE), EDGE), :]
                        for s in range(OWN):
                            want = slots[target, s] if flip else s
                            acc[s] = acc[s] + val * (slot == want).astype(jnp.float32)
                sums.append(acc)
            for s in range(OWN):
                total = sums[0][s] + flipped(sums[1][s])
                before = befores[j * OWN + s]
                if before is not None:
                    total = total + before[a]
                outs[j * OWN + s][a] = total
            return carry

        lax.fori_loop(0, HIGH, dest, 0)


def signed(axis_size, distance):
    pairs = []
    for i in range(axis_size):
        for c in range(2):
            step = distance if c == 0 else -distance
            pairs.append((i * 2 + c, (i + step) % axis_size * 2 + c))
    return pairs


def move_x(array, distance):
    return lax.ppermute(array, ("x", "c"), signed(NX, distance))


def move_z(array, distance):
    return lax.ppermute(array, ("h", "l", "c"), signed(NZ, distance))


def gather(slots, arrays, before=()):
    n = len(arrays)
    cells = OWN * len(NEAR)
    return pl.pallas_call(
        functools.partial(gather_kernel, n, len(before) > 0),
        out_shape=[jax.ShapeDtypeStruct((HIGH, EDGE, EDGE), jnp.float32)] * cells,
        in_specs=sm(1) + vm(n + len(before)),
        out_specs=vm(cells),
        scratch_shapes=[pltpu.SMEM((n, TABLE, EDGE), jnp.float32), pltpu.SemaphoreType.DMA((n,))],
        name="gather_more" if before else "gather",
    )(slots, *[pltpu.with_memory_space_constraint(a, VMEM) for a in (*arrays, *before)])


def vm(n):
    return [pl.BlockSpec(memory_space=VMEM)] * n


def sm(n):
    return [pl.BlockSpec(memory_space=SMEM)] * n


def body(
    t2_tiles,
    cycle_ints,
    cycle_left,
    cycle_right,
    cycle_dest,
    lam_ladder,
    ladder_ints,
    ladder_mask,
    partner_slot,
    denom,
):
    f32 = jnp.float32
    payload = pl.pallas_call(
        products_kernel,
        out_shape=jax.ShapeDtypeStruct((ROWS, EDGE), f32),
        in_specs=sm(3) + vm(2),
        out_specs=pl.BlockSpec(memory_space=VMEM),
        scratch_shapes=[pltpu.SMEM((NX * NZ,), jnp.int32)],
        name="products",
    )(cycle_left[0, 0], cycle_right[0, 0], cycle_dest[0, 0], t2_tiles[0, 0], cycle_ints[0, 0])
    got_a = move_x(payload, 1)
    got_b = move_x(payload, -1)
    partial = pl.pallas_call(
        ladder_kernel,
        out_shape=jax.ShapeDtypeStruct((8, OWN * EDGE, EDGE), f32),
        in_specs=sm(1) + vm(2),
        out_specs=pl.BlockSpec(memory_space=VMEM),
        name="ladder",
    )(ladder_mask, lam_ladder, ladder_ints)
    own_slots = jnp.broadcast_to(partner_slot[0], (NZ, 32, OWN)) if 32 == 1 else jnp.broadcast_to(
        jnp.pad(partner_slot, ((0, 0), (0, EDGE - OWN))), (NZ, 32, EDGE)
    )
    slots = lax.all_to_all(own_slots, ("h", "l"), split_axis=0, concat_axis=0, tiled=True)
    slots = slots[:, 0, :OWN]
    got_a, got_b, partial = lax.optimization_barrier((got_a, got_b, partial))
    got_c = move_x(got_a, 1)

    near = gather(slots, (payload, got_a, got_b))
    near, partial = lax.optimization_barrier((near, partial))
    spread = lax.all_to_all(partial, ("y", "c"), split_axis=0, concat_axis=0, tiled=True)
    ladder = jnp.sum(spread, axis=0)
    n_occ = NX * NZ
    mirror = [(i, n_occ - 1 - i) for i in range(n_occ)]
    other = lax.ppermute(ladder, ("x", "h", "l"), mirror)

    near = gather(slots, (got_c,), near)
    halves_done = []
    for s in range(OWN):
        cells = near[s::OWN]
        far = cells[3]
        for j in range(3):
            far = far + move_z(cells[j], NEAR[j])
        if s == OWN - 1:
            far, other = lax.optimization_barrier((far, other))
        far = lax.all_to_all(far, "h", split_axis=0, concat_axis=0, tiled=True)
        halves_done.append(far[0] + far[1] + far[2] + far[3])
    other = other.reshape(OWN, EDGE, EDGE)[partner_slot[0]][:, ::-1, ::-1]
    ladder = ladder + other.reshape(OWN * EDGE, EDGE)
    return (ladder + jnp.concatenate(halves_done, axis=0)) / denom


def solution(mesh):
    grid = Mesh(mesh.devices.reshape(NX, HIGH, LOW, 4, 2), ("x", "h", "l", "y", "c"))
    occ = ("x", "h", "l")
    vir = ("y", "c")
    in_specs = (
        P(occ, vir, None, None, None),
        P(occ, vir, None, None, None),
        P(occ, vir, None),
        P(occ, vir, None),
        P(occ, vir, None),
        P(occ, vir),
        P(vir, None),
        P(occ, vir),
        P(occ, None),
        P(occ, vir),
    )
    return jax.shard_map(
        body, mesh=grid, in_specs=in_specs, out_specs=P(occ, vir), check_vma=False
    )
```

```python
import functools

import jax
import jax.numpy as jnp
from jax import lax
from jax.experimental import pallas as pl
from jax.experimental.pallas import tpu as pltpu
from jax.sharding import Mesh
from jax.sharding import PartitionSpec as P

CAP = 3
EDGE = 128
OWN = 2
XT = 4
NX = 4
NZ = 16
TASKS = 96
ENTRIES = NX * NZ * CAP
PAIRS = XT * XT
TABLE = 8
ROWS = PAIRS * EDGE + TABLE
HIGH = 4
LOW = 4
NEAR = (2, 1, -1, 0)
HIGHEST = lax.Precision.HIGHEST
SMEM = pltpu.SMEM
VMEM = pltpu.VMEM


def halves(value):
    high = value.astype(jnp.bfloat16)
    return high, (value - high.astype(jnp.float32)).astype(jnp.bfloat16)


def dot3(left, right):
    left_high, left_low = halves(left)
    right_high, right_low = halves(right)
    dot = functools.partial(jnp.dot, preferred_element_type=jnp.float32)
    return dot(left_high, right_high) + (dot(left_high, right_low) + dot(left_low, right_high))


def products_kernel(lefts, rights, dests, t2_ref, ints_ref, out_ref, count):
    for i in range(NX * NZ):
        count[i] = 0
    where = (
        lax.broadcasted_iota(jnp.int32, (TABLE, EDGE), 0) * EDGE
        + lax.broadcasted_iota(jnp.int32, (TABLE, EDGE), 1)
    )
    table = jnp.full((TABLE, EDGE), -1, jnp.int32)
    for t in range(TASKS):
        dest = dests[t]
        owner = lax.shift_right_logical(dest, 1)
        rank = count[owner]
        count[owner] = rank + 1
        entry = jnp.bitwise_and(dest, OWN - 1) * PAIRS + lefts[t] * XT + rights[t]
        table = jnp.where(where == owner * CAP + rank, entry, table)
    out_ref[PAIRS * EDGE :, :] = table.astype(jnp.float32)
    right = jnp.concatenate([ints_ref[r] for r in range(XT)], axis=1)
    for l in range(XT):
        tile = dot3(t2_ref[l], right)
        for r in range(XT):
            out_ref[pl.ds((l * XT + r) * EDGE, EDGE), :] = tile[:, r * EDGE : (r + 1) * EDGE]


def ladder_kernel(mask, lam_ref, ints_ref, out_ref):
    blocks = lam_ref.shape[1] // EDGE
    for s in range(OWN):
        rows = [
            lam_ref[pl.ds(s * EDGE, EDGE), pl.ds(b * EDGE, EDGE)]
            * mask[s, b].astype(jnp.float32)
            for b in range(blocks)
        ]
        part = dot3(jnp.concatenate(rows, axis=1), ints_ref[...])
        for q in range(out_ref.shape[0]):
            out_ref[q, pl.ds(s * EDGE, EDGE), :] = part[:, q * EDGE : (q + 1) * EDGE]


def flipped(value):
    last = value.shape[0] // 8 - 1
    lane = EDGE - 1 - lax.broadcasted_iota(jnp.int32, (8, EDGE), 1)
    row = 7 - lax.broadcasted_iota(jnp.int32, (8, EDGE), 0)
    parts = []
    for i in range(last + 1):
        part = value[(last - i) * 8 : (last - i + 1) * 8]
        part = jnp.take_along_axis(part, lane, axis=1, mode="promise_in_bounds")
        part = jnp.take_along_axis(part, row, axis=0, mode="promise_in_bounds")
        parts.append(part)
    return jnp.concatenate(parts, axis=0)


def gather_kernel(sources, more, slots, *refs):
    tiles = refs[:sources]
    refs = refs[sources:]
    cells = NEAR
    befores = refs[: len(cells)] if more else (None,) * len(cells)
    refs = refs[len(cells) :] if more else refs
    outs = refs[: len(cells)]
    tables, sems = refs[len(cells) :]
    copies = [
        pltpu.make_async_copy(tile.at[pl.ds(PAIRS * EDGE, TABLE)], tables.at[i], sems.at[i])
        for i, tile in enumerate(tiles)
    ]
    for copy in copies:
        copy.start()
    base = lax.axis_index("x") * NZ
    z = lax.axis_index("h") * LOW + lax.axis_index("l")
    sign = 1 - 2 * lax.axis_index("c")
    for copy in copies:
        copy.wait()
    for j, near in enumerate(NEAR):
        low = jnp.bitwise_and(z + sign * near + NZ, LOW - 1)

        def dest(a, carry, low=low, j=j):
            target = a * LOW + low
            owner = base + target
            sums = []
            for flip in range(2):
                start = (NX * NZ - 1 - owner if flip else owner) * CAP
                acc = [jnp.zeros((EDGE, EDGE), jnp.float32) for _ in range(OWN)]
                for i, tile in enumerate(tiles):
                    for k in range(CAP):
                        at = start + k
                        row = lax.shift_right_logical(at, 7)
                        lane = jnp.bitwise_and(at, EDGE - 1)
                        entry = tables[i, row, lane].astype(jnp.int32)
                        slot = lax.shift_right_arithmetic(entry, 4)
                        code = jnp.bitwise_and(jnp.maximum(entry, 0), PAIRS - 1)
                        val = tile[pl.ds(pl.multiple_of(code * EDGE, EDGE), EDGE), :]
                        for s in range(OWN):
                            want = slots[target, s] if flip else s
                            acc[s] = acc[s] + val * (slot == want).astype(jnp.float32)
                sums.append(acc)
            for s in range(OWN):
                total = sums[0][s] + flipped(sums[1][s])
                rows = pl.ds(s * EDGE, EDGE)
                if befores[j] is not None:
                    total = total + befores[j][a, rows, :]
                outs[j][a, rows, :] = total
            return carry

        lax.fori_loop(0, HIGH, dest, 0)


def signed(axis_size, distance):
    pairs = []
    for i in range(axis_size):
        for c in range(2):
            step = distance if c == 0 else -distance
            pairs.append((i * 2 + c, (i + step) % axis_size * 2 + c))
    return pairs


def move_x(array, distance):
    return lax.ppermute(array, ("x", "c"), signed(NX, distance))


def move_z(array, distance):
    return lax.ppermute(array, ("h", "l", "c"), signed(NZ, distance))


def gather(slots, arrays, before=()):
    n = len(arrays)
    cells = len(NEAR)
    return pl.pallas_call(
        functools.partial(gather_kernel, n, len(before) > 0),
        out_shape=[jax.ShapeDtypeStruct((HIGH, OWN * EDGE, EDGE), jnp.float32)] * cells,
        in_specs=sm(1) + vm(n + len(before)),
        out_specs=vm(cells),
        scratch_shapes=[pltpu.SMEM((n, TABLE, EDGE), jnp.float32), pltpu.SemaphoreType.DMA((n,))],
        name="gather_more" if before else "gather",
    )(slots, *[pltpu.with_memory_space_constraint(a, VMEM) for a in (*arrays, *before)])


def vm(n):
    return [pl.BlockSpec(memory_space=VMEM)] * n


def sm(n):
    return [pl.BlockSpec(memory_space=SMEM)] * n


def body(
    t2_tiles,
    cycle_ints,
    cycle_left,
    cycle_right,
    cycle_dest,
    lam_ladder,
    ladder_ints,
    ladder_mask,
    partner_slot,
    denom,
):
    f32 = jnp.float32
    payload = pl.pallas_call(
        products_kernel,
        out_shape=jax.ShapeDtypeStruct((ROWS, EDGE), f32),
        in_specs=sm(3) + vm(2),
        out_specs=pl.BlockSpec(memory_space=VMEM),
        scratch_shapes=[pltpu.SMEM((NX * NZ,), jnp.int32)],
        name="products",
    )(cycle_left[0, 0], cycle_right[0, 0], cycle_dest[0, 0], t2_tiles[0, 0], cycle_ints[0, 0])
    got_a = move_x(payload, 1)
    got_b = move_x(payload, -1)
    partial = pl.pallas_call(
        ladder_kernel,
        out_shape=jax.ShapeDtypeStruct((8, OWN * EDGE, EDGE), f32),
        in_specs=sm(1) + vm(2),
        out_specs=pl.BlockSpec(memory_space=VMEM),
        name="ladder",
    )(ladder_mask, lam_ladder, ladder_ints)
    own_slots = jnp.pad(partner_slot, ((0, 0), (0, EDGE - OWN)))
    own_slots = jnp.broadcast_to(own_slots, (NZ, 32, EDGE))
    slots = lax.all_to_all(own_slots, ("h", "l"), split_axis=0, concat_axis=0, tiled=True)
    slots = slots[:, 0, :OWN]
    got_a, got_b, partial = lax.optimization_barrier((got_a, got_b, partial))
    got_c = move_x(got_a, 1)

    spread = lax.all_to_all(partial, ("y", "c"), split_axis=0, concat_axis=0, tiled=True)
    near = gather(slots, (payload, got_a, got_b))
    near, spread = lax.optimization_barrier((near, spread))
    ladder = jnp.sum(spread, axis=0)
    n_occ = NX * NZ
    mirror = [(i, n_occ - 1 - i) for i in range(n_occ)]
    other = lax.ppermute(ladder, ("x", "h", "l"), mirror)
    near, ladder = lax.optimization_barrier((near, ladder))
    near = gather(slots, (got_c,), near)
    near, other = lax.optimization_barrier((near, other))
    moved = [move_z(near[j], NEAR[j]) for j in range(3)]
    far = near[3] + moved[0] + moved[1] + moved[2]
    far = lax.all_to_all(far, "h", split_axis=0, concat_axis=0, tiled=True)
    other = other.reshape(OWN, EDGE, EDGE)[partner_slot[0]][:, ::-1, ::-1]
    ladder = ladder + other.reshape(OWN * EDGE, EDGE)
    return (ladder + far[0] + far[1] + far[2] + far[3]) / denom


def solution(mesh):
    grid = Mesh(mesh.devices.reshape(NX, HIGH, LOW, 4, 2), ("x", "h", "l", "y", "c"))
    occ = ("x", "h", "l")
    vir = ("y", "c")
    in_specs = (
        P(occ, vir, None, None, None),
        P(occ, vir, None, None, None),
        P(occ, vir, None),
        P(occ, vir, None),
        P(occ, vir, None),
        P(occ, vir),
        P(vir, None),
        P(occ, vir),
        P(occ, None),
        P(occ, vir),
    )
    return jax.shard_map(
        body, mesh=grid, in_specs=in_specs, out_specs=P(occ, vir), check_vma=False
    )
```

```python
import functools

import jax
import jax.numpy as jnp
from jax import lax
from jax.experimental import pallas as pl
from jax.experimental.pallas import tpu as pltpu
from jax.sharding import Mesh
from jax.sharding import PartitionSpec as P

CAP = 3
EDGE = 128
OWN = 2
XT = 4
NX = 4
NZ = 16
TASKS = 96
ENTRIES = NX * NZ * CAP
PAIRS = XT * XT
TABLE = 8
ROWS = PAIRS * EDGE + TABLE
HIGH = 4
LOW = 4
NEAR = (2, 1, -1, 0)
HIGHEST = lax.Precision.HIGHEST
SMEM = pltpu.SMEM
VMEM = pltpu.VMEM


def halves(value):
    high = value.astype(jnp.bfloat16)
    return high, (value - high.astype(jnp.float32)).astype(jnp.bfloat16)


def dot3(left, right):
    left_high, left_low = halves(left)
    right_high, right_low = halves(right)
    dot = functools.partial(jnp.dot, preferred_element_type=jnp.float32)
    return dot(left_high, right_high) + (dot(left_high, right_low) + dot(left_low, right_high))


def products_kernel(lefts, rights, dests, t2_ref, ints_ref, out_ref, count):
    for i in range(NX * NZ):
        count[i] = 0
    where = (
        lax.broadcasted_iota(jnp.int32, (TABLE, EDGE), 0) * EDGE
        + lax.broadcasted_iota(jnp.int32, (TABLE, EDGE), 1)
    )
    table = jnp.full((TABLE, EDGE), -1, jnp.int32)
    for t in range(TASKS):
        dest = dests[t]
        owner = lax.shift_right_logical(dest, 1)
        rank = count[owner]
        count[owner] = rank + 1
        entry = jnp.bitwise_and(dest, OWN - 1) * PAIRS + lefts[t] * XT + rights[t]
        table = jnp.where(where == owner * CAP + rank, entry, table)
    out_ref[PAIRS * EDGE :, :] = table.astype(jnp.float32)
    right = jnp.concatenate([ints_ref[r] for r in range(XT)], axis=1)
    for l in range(XT):
        tile = dot3(t2_ref[l], right)
        for r in range(XT):
            out_ref[pl.ds((l * XT + r) * EDGE, EDGE), :] = tile[:, r * EDGE : (r + 1) * EDGE]


def ladder_kernel(mask, lam_ref, ints_ref, out_ref):
    blocks = lam_ref.shape[1] // EDGE
    for s in range(OWN):
        rows = [
            lam_ref[pl.ds(s * EDGE, EDGE), pl.ds(b * EDGE, EDGE)]
            * mask[s, b].astype(jnp.float32)
            for b in range(blocks)
        ]
        part = dot3(jnp.concatenate(rows, axis=1), ints_ref[...])
        for q in range(out_ref.shape[0]):
            out_ref[q, pl.ds(s * EDGE, EDGE), :] = part[:, q * EDGE : (q + 1) * EDGE]


def flipped(value):
    last = value.shape[0] // 8 - 1
    lane = EDGE - 1 - lax.broadcasted_iota(jnp.int32, (8, EDGE), 1)
    row = 7 - lax.broadcasted_iota(jnp.int32, (8, EDGE), 0)
    parts = []
    for i in range(last + 1):
        part = value[(last - i) * 8 : (last - i + 1) * 8]
        part = jnp.take_along_axis(part, lane, axis=1, mode="promise_in_bounds")
        part = jnp.take_along_axis(part, row, axis=0, mode="promise_in_bounds")
        parts.append(part)
    return jnp.concatenate(parts, axis=0)


def gather_kernel(sources, more, slots, *refs):
    tiles = refs[:sources]
    refs = refs[sources:]
    cells = NEAR
    befores = refs[: len(cells)] if more else (None,) * len(cells)
    refs = refs[len(cells) :] if more else refs
    outs = refs[: len(cells)]
    tables, sems = refs[len(cells) :]
    copies = [
        pltpu.make_async_copy(tile.at[pl.ds(PAIRS * EDGE, TABLE)], tables.at[i], sems.at[i])
        for i, tile in enumerate(tiles)
    ]
    for copy in copies:
        copy.start()
    base = lax.axis_index("x") * NZ
    z = lax.axis_index("h") * LOW + lax.axis_index("l")
    sign = 1 - 2 * lax.axis_index("c")
    for copy in copies:
        copy.wait()
    for j, near in enumerate(NEAR):
        via = jnp.bitwise_and(z + sign * near + NZ, NZ - 1)

        def dest(a, carry, via=via, j=j):
            target = jnp.bitwise_and(via + sign * LOW * a + NZ, NZ - 1)
            owner = base + target
            sums = []
            for flip in range(2):
                start = (NX * NZ - 1 - owner if flip else owner) * CAP
                acc = [jnp.zeros((EDGE, EDGE), jnp.float32) for _ in range(OWN)]
                for i, tile in enumerate(tiles):
                    for k in range(CAP):
                        at = start + k
                        row = lax.shift_right_logical(at, 7)
                        lane = jnp.bitwise_and(at, EDGE - 1)
                        entry = tables[i, row, lane].astype(jnp.int32)
                        slot = lax.shift_right_arithmetic(entry, 4)
                        code = jnp.bitwise_and(jnp.maximum(entry, 0), PAIRS - 1)
                        val = tile[pl.ds(pl.multiple_of(code * EDGE, EDGE), EDGE), :]
                        for s in range(OWN):
                            want = slots[target, s] if flip else s
                            acc[s] = acc[s] + val * (slot == want).astype(jnp.float32)
                sums.append(acc)
            for s in range(OWN):
                total = sums[0][s] + flipped(sums[1][s])
                rows = pl.ds(s * EDGE, EDGE)
                if befores[j] is not None:
                    total = total + befores[j][a, rows, :]
                outs[j][a, rows, :] = total
            return carry

        lax.fori_loop(0, HIGH, dest, 0)


def signed(axis_size, distance):
    pairs = []
    for i in range(axis_size):
        for c in range(2):
            step = distance if c == 0 else -distance
            pairs.append((i * 2 + c, (i + step) % axis_size * 2 + c))
    return pairs


def move_x(array, distance):
    return lax.ppermute(array, ("x", "c"), signed(NX, distance))


def move_z(array, distance):
    return lax.ppermute(array, ("h", "l", "c"), signed(NZ, distance))


def gather(slots, arrays, before=()):
    n = len(arrays)
    cells = len(NEAR)
    return pl.pallas_call(
        functools.partial(gather_kernel, n, len(before) > 0),
        out_shape=[jax.ShapeDtypeStruct((HIGH, OWN * EDGE, EDGE), jnp.float32)] * cells,
        in_specs=sm(1) + vm(n + len(before)),
        out_specs=vm(cells),
        scratch_shapes=[pltpu.SMEM((n, TABLE, EDGE), jnp.float32), pltpu.SemaphoreType.DMA((n,))],
        name="gather_more" if before else "gather",
    )(slots, *[pltpu.with_memory_space_constraint(a, VMEM) for a in (*arrays, *before)])


def vm(n):
    return [pl.BlockSpec(memory_space=VMEM)] * n


def sm(n):
    return [pl.BlockSpec(memory_space=SMEM)] * n


def body(
    t2_tiles,
    cycle_ints,
    cycle_left,
    cycle_right,
    cycle_dest,
    lam_ladder,
    ladder_ints,
    ladder_mask,
    partner_slot,
    denom,
):
    f32 = jnp.float32
    payload = pl.pallas_call(
        products_kernel,
        out_shape=jax.ShapeDtypeStruct((ROWS, EDGE), f32),
        in_specs=sm(3) + vm(2),
        out_specs=pl.BlockSpec(memory_space=VMEM),
        scratch_shapes=[pltpu.SMEM((NX * NZ,), jnp.int32)],
        name="products",
    )(cycle_left[0, 0], cycle_right[0, 0], cycle_dest[0, 0], t2_tiles[0, 0], cycle_ints[0, 0])
    got_a = move_x(payload, 1)
    got_b = move_x(payload, -1)
    partial = pl.pallas_call(
        ladder_kernel,
        out_shape=jax.ShapeDtypeStruct((8, OWN * EDGE, EDGE), f32),
        in_specs=sm(1) + vm(2),
        out_specs=pl.BlockSpec(memory_space=VMEM),
        name="ladder",
    )(ladder_mask, lam_ladder, ladder_ints)
    own_slots = jnp.pad(partner_slot, ((0, 0), (0, EDGE - OWN)))
    own_slots = jnp.broadcast_to(own_slots, (NZ, 32, EDGE))
    slots = lax.all_to_all(own_slots, ("h", "l"), split_axis=0, concat_axis=0, tiled=True)
    slots = slots[:, 0, :OWN]
    got_a, got_b, partial = lax.optimization_barrier((got_a, got_b, partial))
    got_c = move_x(got_a, 1)

    near = gather(slots, (payload, got_a, got_b))
    near, partial = lax.optimization_barrier((near, partial))
    spread = lax.all_to_all(partial, ("y", "c"), split_axis=0, concat_axis=0, tiled=True)
    ladder = jnp.sum(spread, axis=0)
    n_occ = NX * NZ
    mirror = [(i, n_occ - 1 - i) for i in range(n_occ)]
    other = lax.ppermute(ladder, ("x", "h", "l"), mirror)

    near = gather(slots, (got_c,), near)
    moved = [move_z(near[j], NEAR[j]) for j in range(3)]
    far = near[3] + moved[0] + moved[1] + moved[2]
    far, other = lax.optimization_barrier((far, other))
    far = [far[0]] + [move_z(far[a], LOW * a) for a in (2, 1, 3)]
    other = other.reshape(OWN, EDGE, EDGE)[partner_slot[0]][:, ::-1, ::-1]
    ladder = ladder + other.reshape(OWN * EDGE, EDGE)
    return (ladder + far[0] + far[1] + far[2] + far[3]) / denom


def solution(mesh):
    grid = Mesh(mesh.devices.reshape(NX, HIGH, LOW, 4, 2), ("x", "h", "l", "y", "c"))
    occ = ("x", "h", "l")
    vir = ("y", "c")
    in_specs = (
        P(occ, vir, None, None, None),
        P(occ, vir, None, None, None),
        P(occ, vir, None),
        P(occ, vir, None),
        P(occ, vir, None),
        P(occ, vir),
        P(vir, None),
        P(occ, vir),
        P(occ, None),
        P(occ, vir),
    )
    return jax.shard_map(
        body, mesh=grid, in_specs=in_specs, out_specs=P(occ, vir), check_vma=False
    )
```

```python
import functools

import jax
import jax.numpy as jnp
from jax import lax
from jax.experimental import pallas as pl
from jax.experimental.pallas import tpu as pltpu
from jax.sharding import Mesh
from jax.sharding import PartitionSpec as P

CAP = 3
EDGE = 128
OWN = 2
XT = 4
NX = 4
NZ = 16
TASKS = 96
ENTRIES = NX * NZ * CAP
PAIRS = XT * XT
TABLE = 8
ROWS = PAIRS * EDGE + TABLE
HIGH = 4
LOW = 4
NEAR = (2, 1, -1, 0)
HIGHEST = lax.Precision.HIGHEST
SMEM = pltpu.SMEM
VMEM = pltpu.VMEM


def halves(value):
    high = value.astype(jnp.bfloat16)
    return high, (value - high.astype(jnp.float32)).astype(jnp.bfloat16)


def dot3(left, right):
    left_high, left_low = halves(left)
    right_high, right_low = halves(right)
    dot = functools.partial(jnp.dot, preferred_element_type=jnp.float32)
    return dot(left_high, right_high) + (dot(left_high, right_low) + dot(left_low, right_high))


def products_kernel(lefts, rights, dests, t2_ref, ints_ref, out_ref, count):
    for i in range(NX * NZ):
        count[i] = 0
    where = (
        lax.broadcasted_iota(jnp.int32, (TABLE, EDGE), 0) * EDGE
        + lax.broadcasted_iota(jnp.int32, (TABLE, EDGE), 1)
    )
    table = jnp.full((TABLE, EDGE), -1, jnp.int32)
    for t in range(TASKS):
        dest = dests[t]
        owner = lax.shift_right_logical(dest, 1)
        rank = count[owner]
        count[owner] = rank + 1
        entry = jnp.bitwise_and(dest, OWN - 1) * PAIRS + lefts[t] * XT + rights[t]
        table = jnp.where(where == owner * CAP + rank, entry, table)
    out_ref[PAIRS * EDGE :, :] = table.astype(jnp.float32)
    right = jnp.concatenate([ints_ref[r] for r in range(XT)], axis=1)
    for l in range(XT):
        tile = dot3(t2_ref[l], right)
        for r in range(XT):
            out_ref[pl.ds((l * XT + r) * EDGE, EDGE), :] = tile[:, r * EDGE : (r + 1) * EDGE]


def ladder_kernel(mask, lam_ref, ints_ref, out_ref):
    blocks = lam_ref.shape[1] // EDGE
    for s in range(OWN):
        rows = [
            lam_ref[pl.ds(s * EDGE, EDGE), pl.ds(b * EDGE, EDGE)]
            * mask[s, b].astype(jnp.float32)
            for b in range(blocks)
        ]
        part = dot3(jnp.concatenate(rows, axis=1), ints_ref[...])
        for q in range(out_ref.shape[0]):
            out_ref[q, pl.ds(s * EDGE, EDGE), :] = part[:, q * EDGE : (q + 1) * EDGE]


def flipped(value):
    last = value.shape[0] // 8 - 1
    lane = EDGE - 1 - lax.broadcasted_iota(jnp.int32, (8, EDGE), 1)
    row = 7 - lax.broadcasted_iota(jnp.int32, (8, EDGE), 0)
    parts = []
    for i in range(last + 1):
        part = value[(last - i) * 8 : (last - i + 1) * 8]
        part = jnp.take_along_axis(part, lane, axis=1, mode="promise_in_bounds")
        part = jnp.take_along_axis(part, row, axis=0, mode="promise_in_bounds")
        parts.append(part)
    return jnp.concatenate(parts, axis=0)


def gather_kernel(sources, more, slots, *refs):
    tiles = refs[:sources]
    refs = refs[sources:]
    cells = NEAR
    befores = refs[: len(cells)] if more else (None,) * len(cells)
    refs = refs[len(cells) :] if more else refs
    outs = refs[: len(cells)]
    tables, sems = refs[len(cells) :]
    copies = [
        pltpu.make_async_copy(tile.at[pl.ds(PAIRS * EDGE, TABLE)], tables.at[i], sems.at[i])
        for i, tile in enumerate(tiles)
    ]
    for copy in copies:
        copy.start()
    base = lax.axis_index("x") * NZ
    z = lax.axis_index("h") * LOW + lax.axis_index("l")
    sign = 1 - 2 * lax.axis_index("c")
    for copy in copies:
        copy.wait()
    for j, near in enumerate(NEAR):
        via = jnp.bitwise_and(z + sign * near + NZ, NZ - 1)

        def dest(a, carry, via=via, j=j):
            target = jnp.bitwise_and(via + sign * LOW * a + NZ, NZ - 1)
            owner = base + target
            sums = []
            for flip in range(2):
                start = (NX * NZ - 1 - owner if flip else owner) * CAP
                acc = [jnp.zeros((EDGE, EDGE), jnp.float32) for _ in range(OWN)]
                for i, tile in enumerate(tiles):
                    for k in range(CAP):
                        at = start + k
                        row = lax.shift_right_logical(at, 7)
                        lane = jnp.bitwise_and(at, EDGE - 1)
                        entry = tables[i, row, lane].astype(jnp.int32)
                        slot = lax.shift_right_arithmetic(entry, 4)
                        code = jnp.bitwise_and(jnp.maximum(entry, 0), PAIRS - 1)
                        val = tile[pl.ds(pl.multiple_of(code * EDGE, EDGE), EDGE), :]
                        for s in range(OWN):
                            want = slots[target, s] if flip else s
                            acc[s] = acc[s] + val * (slot == want).astype(jnp.float32)
                sums.append(acc)
            for s in range(OWN):
                total = sums[0][s] + flipped(sums[1][s])
                rows = pl.ds(s * EDGE, EDGE)
                if befores[j] is not None:
                    total = total + befores[j][a, rows, :]
                outs[j][a, rows, :] = total
            return carry

        lax.fori_loop(0, HIGH, dest, 0, unroll=True)


def signed(axis_size, distance):
    pairs = []
    for i in range(axis_size):
        for c in range(2):
            step = distance if c == 0 else -distance
            pairs.append((i * 2 + c, (i + step) % axis_size * 2 + c))
    return pairs


def move_x(array, distance):
    return lax.ppermute(array, ("x", "c"), signed(NX, distance))


def move_z(array, distance):
    return lax.ppermute(array, ("h", "l", "c"), signed(NZ, distance))


def gather(slots, arrays, before=()):
    n = len(arrays)
    cells = len(NEAR)
    return pl.pallas_call(
        functools.partial(gather_kernel, n, len(before) > 0),
        out_shape=[jax.ShapeDtypeStruct((HIGH, OWN * EDGE, EDGE), jnp.float32)] * cells,
        in_specs=sm(1) + vm(n + len(before)),
        out_specs=vm(cells),
        scratch_shapes=[pltpu.SMEM((n, TABLE, EDGE), jnp.float32), pltpu.SemaphoreType.DMA((n,))],
        name="gather_more" if before else "gather",
    )(slots, *[pltpu.with_memory_space_constraint(a, VMEM) for a in (*arrays, *before)])


def vm(n):
    return [pl.BlockSpec(memory_space=VMEM)] * n


def sm(n):
    return [pl.BlockSpec(memory_space=SMEM)] * n


def body(
    t2_tiles,
    cycle_ints,
    cycle_left,
    cycle_right,
    cycle_dest,
    lam_ladder,
    ladder_ints,
    ladder_mask,
    partner_slot,
    denom,
):
    f32 = jnp.float32
    payload = pl.pallas_call(
        products_kernel,
        out_shape=jax.ShapeDtypeStruct((ROWS, EDGE), f32),
        in_specs=sm(3) + vm(2),
        out_specs=pl.BlockSpec(memory_space=VMEM),
        scratch_shapes=[pltpu.SMEM((NX * NZ,), jnp.int32)],
        name="products",
    )(cycle_left[0, 0], cycle_right[0, 0], cycle_dest[0, 0], t2_tiles[0, 0], cycle_ints[0, 0])
    got_a = move_x(payload, 1)
    got_b = move_x(payload, -1)
    partial = pl.pallas_call(
        ladder_kernel,
        out_shape=jax.ShapeDtypeStruct((8, OWN * EDGE, EDGE), f32),
        in_specs=sm(1) + vm(2),
        out_specs=pl.BlockSpec(memory_space=VMEM),
        name="ladder",
    )(ladder_mask, lam_ladder, ladder_ints)
    own_slots = jnp.pad(partner_slot, ((0, 0), (0, EDGE - OWN)))
    own_slots = jnp.broadcast_to(own_slots, (NZ, 24, EDGE))
    slots = lax.all_to_all(own_slots, ("h", "l"), split_axis=0, concat_axis=0, tiled=True)
    slots = slots[:, 0, :OWN]
    got_a, got_b, partial = lax.optimization_barrier((got_a, got_b, partial))
    got_c = move_x(got_a, 1)

    near = gather(slots, (payload, got_a, got_b))
    near, partial = lax.optimization_barrier((near, partial))
    spread = lax.all_to_all(partial, ("y", "c"), split_axis=0, concat_axis=0, tiled=True)
    ladder = jnp.sum(spread, axis=0)
    n_occ = NX * NZ
    mirror = [(i, n_occ - 1 - i) for i in range(n_occ)]
    other = lax.ppermute(ladder, ("x", "h", "l"), mirror)

    near = gather(slots, (got_c,), near)
    moved = [move_z(near[j], NEAR[j]) for j in range(3)]
    far = near[3] + moved[0] + moved[1] + moved[2]
    far, other = lax.optimization_barrier((far, other))
    far = [far[0]] + [move_z(far[a], LOW * a) for a in (2, 1, 3)]
    other = other.reshape(OWN, EDGE, EDGE)[partner_slot[0]][:, ::-1, ::-1]
    ladder = ladder + other.reshape(OWN * EDGE, EDGE)
    return (ladder + far[0] + far[1] + far[2] + far[3]) / denom


def solution(mesh):
    grid = Mesh(mesh.devices.reshape(NX, HIGH, LOW, 4, 2), ("x", "h", "l", "y", "c"))
    occ = ("x", "h", "l")
    vir = ("y", "c")
    in_specs = (
        P(occ, vir, None, None, None),
        P(occ, vir, None, None, None),
        P(occ, vir, None),
        P(occ, vir, None),
        P(occ, vir, None),
        P(occ, vir),
        P(vir, None),
        P(occ, vir),
        P(occ, None),
        P(occ, vir),
    )
    return jax.shard_map(
        body, mesh=grid, in_specs=in_specs, out_specs=P(occ, vir), check_vma=False
    )
```

```python
import functools

import jax
import jax.numpy as jnp
from jax import lax
from jax.experimental import pallas as pl
from jax.experimental.pallas import tpu as pltpu
from jax.sharding import Mesh
from jax.sharding import PartitionSpec as P

CAP = 3
EDGE = 128
OWN = 2
XT = 4
NX = 4
N_VIR = 8
NZ = 16
TASKS = 96
ENTRIES = NX * NZ * CAP
PAIRS = XT * XT
TABLE = 8
ROWS = PAIRS * EDGE + TABLE
HIGH = 4
LOW = 4
NEAR = (2, 1, -1, 0)
HIGHEST = lax.Precision.HIGHEST
SMEM = pltpu.SMEM
VMEM = pltpu.VMEM


def halves(value):
    high = value.astype(jnp.bfloat16)
    return high, (value - high.astype(jnp.float32)).astype(jnp.bfloat16)


def dot3(left, right):
    left_high, left_low = halves(left)
    right_high, right_low = halves(right)
    dot = functools.partial(jnp.dot, preferred_element_type=jnp.float32)
    return dot(left_high, right_high) + (dot(left_high, right_low) + dot(left_low, right_high))


def products_kernel(lefts, rights, dests, t2_ref, ints_ref, out_ref, count):
    for i in range(NX * NZ):
        count[i] = 0
    where = (
        lax.broadcasted_iota(jnp.int32, (TABLE, EDGE), 0) * EDGE
        + lax.broadcasted_iota(jnp.int32, (TABLE, EDGE), 1)
    )
    table = jnp.full((TABLE, EDGE), -1, jnp.int32)
    for t in range(TASKS):
        dest = dests[t]
        owner = lax.shift_right_logical(dest, 1)
        rank = count[owner]
        count[owner] = rank + 1
        entry = jnp.bitwise_and(dest, OWN - 1) * PAIRS + lefts[t] * XT + rights[t]
        table = jnp.where(where == owner * CAP + rank, entry, table)
    out_ref[PAIRS * EDGE :, :] = table.astype(jnp.float32)
    right = jnp.concatenate([ints_ref[r] for r in range(XT)], axis=1)
    for l in range(XT):
        tile = dot3(t2_ref[l], right)
        for r in range(XT):
            out_ref[pl.ds((l * XT + r) * EDGE, EDGE), :] = tile[:, r * EDGE : (r + 1) * EDGE]


def ladder_kernel(mask, behind, ahead, lam_ref, ints_ref, out_ref):
    blocks = lam_ref.shape[1] // EDGE
    lane = lax.broadcasted_iota(jnp.int32, (TABLE, EDGE), 1)
    extra = jnp.zeros((TABLE, EDGE), jnp.int32)
    for s in range(OWN):
        extra = jnp.where(lane == s, behind[0, s], extra)
        extra = jnp.where(lane == OWN + s, ahead[0, s], extra)
    for q in range(out_ref.shape[0]):
        out_ref[q, pl.ds(OWN * EDGE, TABLE), :] = extra.astype(jnp.float32)
    for s in range(OWN):
        rows = [
            lam_ref[pl.ds(s * EDGE, EDGE), pl.ds(b * EDGE, EDGE)]
            * mask[s, b].astype(jnp.float32)
            for b in range(blocks)
        ]
        part = dot3(jnp.concatenate(rows, axis=1), ints_ref[...])
        for q in range(out_ref.shape[0]):
            out_ref[q, pl.ds(s * EDGE, EDGE), :] = part[:, q * EDGE : (q + 1) * EDGE]


def flipped(value):
    last = value.shape[0] // 8 - 1
    lane = EDGE - 1 - lax.broadcasted_iota(jnp.int32, (8, EDGE), 1)
    row = 7 - lax.broadcasted_iota(jnp.int32, (8, EDGE), 0)
    parts = []
    for i in range(last + 1):
        part = value[(last - i) * 8 : (last - i + 1) * 8]
        part = jnp.take_along_axis(part, lane, axis=1, mode="promise_in_bounds")
        part = jnp.take_along_axis(part, row, axis=0, mode="promise_in_bounds")
        parts.append(part)
    return jnp.concatenate(parts, axis=0)


def gather_kernel(sources, more, mine, others, *refs):
    tiles = refs[:sources]
    refs = refs[sources:]
    cells = NEAR
    befores = refs[: len(cells)] if more else (None,) * len(cells)
    refs = refs[len(cells) :] if more else refs
    outs = refs[: len(cells)]
    tables, sems = refs[len(cells) :]
    copies = [
        pltpu.make_async_copy(tile.at[pl.ds(PAIRS * EDGE, TABLE)], tables.at[i], sems.at[i])
        for i, tile in enumerate(tiles)
    ]
    for copy in copies:
        copy.start()
    base = lax.axis_index("x") * NZ
    z = lax.axis_index("h") * LOW + lax.axis_index("l")
    sign = 1 - 2 * lax.axis_index("c")
    for copy in copies:
        copy.wait()
    for j, near in enumerate(NEAR):
        via = jnp.bitwise_and(z + sign * near + NZ, NZ - 1)

        def dest(a, carry, via=via, j=j):
            target = jnp.bitwise_and(via + sign * LOW * a + NZ, NZ - 1)
            owner = base + target
            step = jnp.bitwise_and(target - z + NZ, NZ - 1)
            near_ahead = step <= N_VIR
            row = jnp.where(near_ahead, jnp.maximum(step - 1, 0), NZ - 1 - step)
            first = jnp.where(near_ahead, OWN, 0)
            slots = [
                jnp.where(step == 0, mine[0, s], others[row, first + s].astype(jnp.int32))
                for s in range(OWN)
            ]
            sums = []
            for flip in range(2):
                start = (NX * NZ - 1 - owner if flip else owner) * CAP
                acc = [jnp.zeros((EDGE, EDGE), jnp.float32) for _ in range(OWN)]
                for i, tile in enumerate(tiles):
                    for k in range(CAP):
                        at = start + k
                        line = lax.shift_right_logical(at, 7)
                        lane = jnp.bitwise_and(at, EDGE - 1)
                        entry = tables[i, line, lane].astype(jnp.int32)
                        slot = lax.shift_right_arithmetic(entry, 4)
                        code = jnp.bitwise_and(jnp.maximum(entry, 0), PAIRS - 1)
                        val = tile[pl.ds(pl.multiple_of(code * EDGE, EDGE), EDGE), :]
                        for s in range(OWN):
                            want = slots[s] if flip else s
                            acc[s] = acc[s] + val * (slot == want).astype(jnp.float32)
                sums.append(acc)
            for s in range(OWN):
                total = sums[0][s] + flipped(sums[1][s])
                rows = pl.ds(s * EDGE, EDGE)
                if befores[j] is not None:
                    total = total + befores[j][a, rows, :]
                outs[j][a, rows, :] = total
            return carry

        lax.fori_loop(0, HIGH, dest, 0, unroll=True)


def signed(axis_size, distance):
    pairs = []
    for i in range(axis_size):
        for c in range(2):
            step = distance if c == 0 else -distance
            pairs.append((i * 2 + c, (i + step) % axis_size * 2 + c))
    return pairs


def move_x(array, distance):
    return lax.ppermute(array, ("x", "c"), signed(NX, distance))


def move_z(array, distance):
    return lax.ppermute(array, ("h", "l", "c"), signed(NZ, distance))


def gather(mine, others, arrays, before=()):
    n = len(arrays)
    cells = len(NEAR)
    return pl.pallas_call(
        functools.partial(gather_kernel, n, len(before) > 0),
        out_shape=[jax.ShapeDtypeStruct((HIGH, OWN * EDGE, EDGE), jnp.float32)] * cells,
        in_specs=sm(2) + vm(n + len(before)),
        out_specs=vm(cells),
        scratch_shapes=[pltpu.SMEM((n, TABLE, EDGE), jnp.float32), pltpu.SemaphoreType.DMA((n,))],
        name="gather_more" if before else "gather",
    )(mine, others, *[pltpu.with_memory_space_constraint(a, VMEM) for a in (*arrays, *before)])


def fetch(array, sign):
    pairs = []
    for i in range(NZ):
        for v in range(N_VIR):
            pairs.append((i * N_VIR + v, (i + sign * (v + 1)) % NZ * N_VIR + v))
    return lax.ppermute(array, ("h", "l", "y", "c"), pairs)


def vm(n):
    return [pl.BlockSpec(memory_space=VMEM)] * n


def sm(n):
    return [pl.BlockSpec(memory_space=SMEM)] * n


def body(
    t2_tiles,
    cycle_ints,
    cycle_left,
    cycle_right,
    cycle_dest,
    lam_ladder,
    ladder_ints,
    ladder_mask,
    partner_slot,
    denom,
):
    f32 = jnp.float32
    payload = pl.pallas_call(
        products_kernel,
        out_shape=jax.ShapeDtypeStruct((ROWS, EDGE), f32),
        in_specs=sm(3) + vm(2),
        out_specs=pl.BlockSpec(memory_space=VMEM),
        scratch_shapes=[pltpu.SMEM((NX * NZ,), jnp.int32)],
        name="products",
    )(cycle_left[0, 0], cycle_right[0, 0], cycle_dest[0, 0], t2_tiles[0, 0], cycle_ints[0, 0])
    got_a = move_x(payload, 1)
    got_b = move_x(payload, -1)
    row, payload = lax.optimization_barrier((partner_slot, payload))
    behind = fetch(row, 1)
    ahead = fetch(row, -1)
    partial = pl.pallas_call(
        ladder_kernel,
        out_shape=jax.ShapeDtypeStruct((N_VIR, OWN * EDGE + TABLE, EDGE), f32),
        in_specs=sm(3) + vm(2),
        out_specs=pl.BlockSpec(memory_space=VMEM),
        name="ladder",
    )(ladder_mask, behind, ahead, lam_ladder, ladder_ints)
    spread = lax.all_to_all(partial, ("y", "c"), split_axis=0, concat_axis=0, tiled=True)
    got_a, got_b, partial = lax.optimization_barrier((got_a, got_b, partial))
    got_c = move_x(got_a, 1)

    others = spread[:, OWN * EDGE, :]
    ladder = jnp.sum(spread[:, : OWN * EDGE], axis=0)
    got_b, ladder = lax.optimization_barrier((got_b, ladder))
    n_occ = NX * NZ
    mirror = [(i, n_occ - 1 - i) for i in range(n_occ)]
    other = lax.ppermute(ladder, ("x", "h", "l"), mirror)

    near = gather(partner_slot, others, (payload, got_a, got_b))
    near = gather(partner_slot, others, (got_c,), near)
    near, other = lax.optimization_barrier((near, other))
    moved = [move_z(near[j], NEAR[j]) for j in range(3)]
    far = near[3] + moved[0] + moved[1] + moved[2]
    far = [far[0]] + [move_z(far[a], LOW * a) for a in (2, 1, 3)]
    other = other.reshape(OWN, EDGE, EDGE)[partner_slot[0]][:, ::-1, ::-1]
    ladder = ladder + other.reshape(OWN * EDGE, EDGE)
    return (ladder + far[0] + far[1] + far[2] + far[3]) / denom


def solution(mesh):
    grid = Mesh(mesh.devices.reshape(NX, HIGH, LOW, 4, 2), ("x", "h", "l", "y", "c"))
    occ = ("x", "h", "l")
    vir = ("y", "c")
    in_specs = (
        P(occ, vir, None, None, None),
        P(occ, vir, None, None, None),
        P(occ, vir, None),
        P(occ, vir, None),
        P(occ, vir, None),
        P(occ, vir),
        P(vir, None),
        P(occ, vir),
        P(occ, None),
        P(occ, vir),
    )
    return jax.shard_map(
        body, mesh=grid, in_specs=in_specs, out_specs=P(occ, vir), check_vma=False
    )
```

```python
import functools

import jax
import jax.numpy as jnp
from jax import lax
from jax.experimental import pallas as pl
from jax.experimental.pallas import tpu as pltpu
from jax.sharding import Mesh
from jax.sharding import PartitionSpec as P

CAP = 3
EDGE = 128
OWN = 2
XT = 4
NX = 4
NZ = 16
TASKS = 96
ENTRIES = NX * NZ * CAP
PAIRS = XT * XT
TABLE = 8
ROWS = PAIRS * EDGE + TABLE
HIGH = 4
LOW = 4
NEAR = (2, 1, -1, 0)
HIGHEST = lax.Precision.HIGHEST
SMEM = pltpu.SMEM
VMEM = pltpu.VMEM


def halves(value):
    high = value.astype(jnp.bfloat16)
    return high, (value - high.astype(jnp.float32)).astype(jnp.bfloat16)


def dot3(left, right):
    left_high, left_low = halves(left)
    right_high, right_low = halves(right)
    dot = functools.partial(jnp.dot, preferred_element_type=jnp.float32)
    return dot(left_high, right_high) + (dot(left_high, right_low) + dot(left_low, right_high))


def products_kernel(lefts, rights, dests, t2_ref, ints_ref, out_ref, count):
    for i in range(NX * NZ):
        count[i] = 0
    where = (
        lax.broadcasted_iota(jnp.int32, (TABLE, EDGE), 0) * EDGE
        + lax.broadcasted_iota(jnp.int32, (TABLE, EDGE), 1)
    )
    table = jnp.full((TABLE, EDGE), -1, jnp.int32)
    for t in range(TASKS):
        dest = dests[t]
        owner = lax.shift_right_logical(dest, 1)
        rank = count[owner]
        count[owner] = rank + 1
        entry = jnp.bitwise_and(dest, OWN - 1) * PAIRS + lefts[t] * XT + rights[t]
        table = jnp.where(where == owner * CAP + rank, entry, table)
    out_ref[PAIRS * EDGE :, :] = table.astype(jnp.float32)
    right = jnp.concatenate([ints_ref[r] for r in range(XT)], axis=1)
    for l in range(XT):
        tile = dot3(t2_ref[l], right)
        for r in range(XT):
            out_ref[pl.ds((l * XT + r) * EDGE, EDGE), :] = tile[:, r * EDGE : (r + 1) * EDGE]


def ladder_kernel(mask, lam_ref, ints_ref, out_ref):
    blocks = lam_ref.shape[1] // EDGE
    for s in range(OWN):
        rows = [
            lam_ref[pl.ds(s * EDGE, EDGE), pl.ds(b * EDGE, EDGE)]
            * mask[s, b].astype(jnp.float32)
            for b in range(blocks)
        ]
        part = dot3(jnp.concatenate(rows, axis=1), ints_ref[...])
        for q in range(out_ref.shape[0]):
            out_ref[q, pl.ds(s * EDGE, EDGE), :] = part[:, q * EDGE : (q + 1) * EDGE]


def flipped(value):
    last = value.shape[0] // 8 - 1
    lane = EDGE - 1 - lax.broadcasted_iota(jnp.int32, (8, EDGE), 1)
    row = 7 - lax.broadcasted_iota(jnp.int32, (8, EDGE), 0)
    parts = []
    for i in range(last + 1):
        part = value[(last - i) * 8 : (last - i + 1) * 8]
        part = jnp.take_along_axis(part, lane, axis=1, mode="promise_in_bounds")
        part = jnp.take_along_axis(part, row, axis=0, mode="promise_in_bounds")
        parts.append(part)
    return jnp.concatenate(parts, axis=0)


def gather_kernel(sources, more, slots, *refs):
    tiles = refs[:sources]
    refs = refs[sources:]
    cells = NEAR
    befores = refs[: len(cells)] if more else (None,) * len(cells)
    refs = refs[len(cells) :] if more else refs
    outs = refs[: len(cells)]
    tables, sems = refs[len(cells) :]
    copies = [
        pltpu.make_async_copy(tile.at[pl.ds(PAIRS * EDGE, TABLE)], tables.at[i], sems.at[i])
        for i, tile in enumerate(tiles)
    ]
    for copy in copies:
        copy.start()
    base = lax.axis_index("x") * NZ
    z = lax.axis_index("h") * LOW + lax.axis_index("l")
    sign = 1 - 2 * lax.axis_index("c")
    for copy in copies:
        copy.wait()
    for j, near in enumerate(NEAR):
        via = jnp.bitwise_and(z + sign * near + NZ, NZ - 1)

        def dest(a, carry, via=via, j=j):
            target = jnp.bitwise_and(via + sign * LOW * a + NZ, NZ - 1)
            owner = base + target
            sums = []
            for flip in range(2):
                start = (NX * NZ - 1 - owner if flip else owner) * CAP
                acc = [jnp.zeros((EDGE, EDGE), jnp.float32) for _ in range(OWN)]
                for i, tile in enumerate(tiles):
                    for k in range(CAP):
                        at = start + k
                        row = lax.shift_right_logical(at, 7)
                        lane = jnp.bitwise_and(at, EDGE - 1)
                        entry = tables[i, row, lane].astype(jnp.int32)
                        slot = lax.shift_right_arithmetic(entry, 4)
                        code = jnp.bitwise_and(jnp.maximum(entry, 0), PAIRS - 1)
                        val = tile[pl.ds(pl.multiple_of(code * EDGE, EDGE), EDGE), :]
                        for s in range(OWN):
                            want = slots[target, s] if flip else s
                            acc[s] = acc[s] + val * (slot == want).astype(jnp.float32)
                sums.append(acc)
            for s in range(OWN):
                total = sums[0][s] + flipped(sums[1][s])
                rows = pl.ds(s * EDGE, EDGE)
                if befores[j] is not None:
                    total = total + befores[j][a, rows, :]
                outs[j][a, rows, :] = total
            return carry

        lax.fori_loop(0, HIGH, dest, 0, unroll=True)


def signed(axis_size, distance):
    pairs = []
    for i in range(axis_size):
        for c in range(2):
            step = distance if c == 0 else -distance
            pairs.append((i * 2 + c, (i + step) % axis_size * 2 + c))
    return pairs


def move_x(array, distance):
    return lax.ppermute(array, ("x", "c"), signed(NX, distance))


def move_z(array, distance):
    return lax.ppermute(array, ("h", "l", "c"), signed(NZ, distance))


def gather(slots, arrays, before=()):
    n = len(arrays)
    cells = len(NEAR)
    return pl.pallas_call(
        functools.partial(gather_kernel, n, len(before) > 0),
        out_shape=[jax.ShapeDtypeStruct((HIGH, OWN * EDGE, EDGE), jnp.float32)] * cells,
        in_specs=sm(1) + vm(n + len(before)),
        out_specs=vm(cells),
        scratch_shapes=[pltpu.SMEM((n, TABLE, EDGE), jnp.float32), pltpu.SemaphoreType.DMA((n,))],
        name="gather_more" if before else "gather",
    )(slots, *[pltpu.with_memory_space_constraint(a, VMEM) for a in (*arrays, *before)])


def vm(n):
    return [pl.BlockSpec(memory_space=VMEM)] * n


def sm(n):
    return [pl.BlockSpec(memory_space=SMEM)] * n


def body(
    t2_tiles,
    cycle_ints,
    cycle_left,
    cycle_right,
    cycle_dest,
    lam_ladder,
    ladder_ints,
    ladder_mask,
    partner_slot,
    denom,
):
    f32 = jnp.float32
    payload = pl.pallas_call(
        products_kernel,
        out_shape=jax.ShapeDtypeStruct((ROWS, EDGE), f32),
        in_specs=sm(3) + vm(2),
        out_specs=pl.BlockSpec(memory_space=VMEM),
        scratch_shapes=[pltpu.SMEM((NX * NZ,), jnp.int32)],
        name="products",
    )(cycle_left[0, 0], cycle_right[0, 0], cycle_dest[0, 0], t2_tiles[0, 0], cycle_ints[0, 0])
    got_a = move_x(payload, 1)
    got_b = move_x(payload, -1)
    partial = pl.pallas_call(
        ladder_kernel,
        out_shape=jax.ShapeDtypeStruct((8, OWN * EDGE, EDGE), f32),
        in_specs=sm(1) + vm(2),
        out_specs=pl.BlockSpec(memory_space=VMEM),
        name="ladder",
    )(ladder_mask, lam_ladder, ladder_ints)
    own_slots = jnp.pad(partner_slot, ((0, 0), (0, EDGE - OWN)))
    own_slots = jnp.broadcast_to(own_slots, (NZ, 24, EDGE))
    slots = lax.all_to_all(own_slots, ("h", "l"), split_axis=0, concat_axis=0, tiled=True)
    slots = slots[:, 0, :OWN]
    got_a, got_b, partial = lax.optimization_barrier((got_a, got_b, partial))
    got_c = move_x(got_a, 1)

    near = gather(slots, (payload, got_a, got_b))
    near, partial = lax.optimization_barrier((near, partial))
    spread = lax.all_to_all(partial, ("y", "c"), split_axis=0, concat_axis=0, tiled=True)
    ladder = jnp.sum(spread, axis=0)
    n_occ = NX * NZ
    mirror = [(i, n_occ - 1 - i) for i in range(n_occ)]
    near = gather(slots, (got_c,), near)
    moved = [move_z(near[j], NEAR[j]) for j in range(3)]
    far = near[3] + moved[0] + moved[1] + moved[2]
    far, ladder = lax.optimization_barrier((far, ladder))
    other = lax.ppermute(ladder, ("x", "h", "l"), mirror)
    far = [far[0]] + [move_z(far[a], LOW * a) for a in (2, 1, 3)]
    far[1], other = lax.optimization_barrier((far[1], other))
    other = other.reshape(OWN, EDGE, EDGE)[partner_slot[0]][:, ::-1, ::-1]
    ladder = ladder + other.reshape(OWN * EDGE, EDGE)
    return (ladder + far[0] + far[1] + far[2] + far[3]) / denom


def solution(mesh):
    grid = Mesh(mesh.devices.reshape(NX, HIGH, LOW, 4, 2), ("x", "h", "l", "y", "c"))
    occ = ("x", "h", "l")
    vir = ("y", "c")
    in_specs = (
        P(occ, vir, None, None, None),
        P(occ, vir, None, None, None),
        P(occ, vir, None),
        P(occ, vir, None),
        P(occ, vir, None),
        P(occ, vir),
        P(vir, None),
        P(occ, vir),
        P(occ, None),
        P(occ, vir),
    )
    return jax.shard_map(
        body, mesh=grid, in_specs=in_specs, out_specs=P(occ, vir), check_vma=False
    )
```

```python
import functools

import jax
import jax.numpy as jnp
from jax import lax
from jax.experimental import pallas as pl
from jax.experimental.pallas import tpu as pltpu
from jax.sharding import Mesh
from jax.sharding import PartitionSpec as P

CAP = 3
EDGE = 128
OWN = 2
XT = 4
NX = 4
NZ = 16
TASKS = 96
ENTRIES = NX * NZ * CAP
PAIRS = XT * XT
TABLE = 8
ROWS = PAIRS * EDGE + TABLE
HIGH = 4
LOW = 4
NEAR = (2, 1, -1, 0)
HIGHEST = lax.Precision.HIGHEST
SMEM = pltpu.SMEM
VMEM = pltpu.VMEM


def halves(value):
    high = value.astype(jnp.bfloat16)
    return high, (value - high.astype(jnp.float32)).astype(jnp.bfloat16)


def dot3(left, right):
    left_high, left_low = halves(left)
    right_high, right_low = halves(right)
    dot = functools.partial(jnp.dot, preferred_element_type=jnp.float32)
    return dot(left_high, right_high) + (dot(left_high, right_low) + dot(left_low, right_high))


def products_kernel(lefts, rights, dests, t2_ref, ints_ref, out_ref, count):
    for i in range(NX * NZ):
        count[i] = 0
    where = (
        lax.broadcasted_iota(jnp.int32, (TABLE, EDGE), 0) * EDGE
        + lax.broadcasted_iota(jnp.int32, (TABLE, EDGE), 1)
    )
    table = jnp.full((TABLE, EDGE), -1, jnp.int32)
    for t in range(TASKS):
        dest = dests[t]
        owner = lax.shift_right_logical(dest, 1)
        rank = count[owner]
        count[owner] = rank + 1
        entry = jnp.bitwise_and(dest, OWN - 1) * PAIRS + lefts[t] * XT + rights[t]
        table = jnp.where(where == owner * CAP + rank, entry, table)
    out_ref[PAIRS * EDGE :, :] = table.astype(jnp.float32)
    right = jnp.concatenate([ints_ref[r] for r in range(XT)], axis=1)
    for l in range(XT):
        tile = dot3(t2_ref[l], right)
        for r in range(XT):
            out_ref[pl.ds((l * XT + r) * EDGE, EDGE), :] = tile[:, r * EDGE : (r + 1) * EDGE]


def ladder_kernel(mask, lam_ref, ints_ref, out_ref):
    blocks = lam_ref.shape[1] // EDGE
    for s in range(OWN):
        rows = [
            lam_ref[pl.ds(s * EDGE, EDGE), pl.ds(b * EDGE, EDGE)]
            * mask[s, b].astype(jnp.float32)
            for b in range(blocks)
        ]
        part = dot3(jnp.concatenate(rows, axis=1), ints_ref[...])
        for q in range(out_ref.shape[0]):
            out_ref[q, pl.ds(s * EDGE, EDGE), :] = part[:, q * EDGE : (q + 1) * EDGE]


def flipped(value):
    last = value.shape[0] // 8 - 1
    lane = EDGE - 1 - lax.broadcasted_iota(jnp.int32, (8, EDGE), 1)
    row = 7 - lax.broadcasted_iota(jnp.int32, (8, EDGE), 0)
    parts = []
    for i in range(last + 1):
        part = value[(last - i) * 8 : (last - i + 1) * 8]
        part = jnp.take_along_axis(part, lane, axis=1, mode="promise_in_bounds")
        part = jnp.take_along_axis(part, row, axis=0, mode="promise_in_bounds")
        parts.append(part)
    return jnp.concatenate(parts, axis=0)


def gather_kernel(sources, more, slots, *refs):
    tiles = refs[:sources]
    refs = refs[sources:]
    cells = NEAR
    befores = refs[: len(cells)] if more else (None,) * len(cells)
    refs = refs[len(cells) :] if more else refs
    outs = refs[: len(cells)]
    tables, sems = refs[len(cells) :]
    copies = [
        pltpu.make_async_copy(tile.at[pl.ds(PAIRS * EDGE, TABLE)], tables.at[i], sems.at[i])
        for i, tile in enumerate(tiles)
    ]
    for copy in copies:
        copy.start()
    base = lax.axis_index("x") * NZ
    z = lax.axis_index("h") * LOW + lax.axis_index("l")
    sign = 1 - 2 * lax.axis_index("c")
    for copy in copies:
        copy.wait()
    for j, near in enumerate(NEAR):
        via = jnp.bitwise_and(z + sign * near + NZ, NZ - 1)

        def dest(a, carry, via=via, j=j):
            target = jnp.bitwise_and(via + sign * LOW * a + NZ, NZ - 1)
            owner = base + target
            sums = []
            for flip in range(2):
                start = (NX * NZ - 1 - owner if flip else owner) * CAP
                acc = [jnp.zeros((EDGE, EDGE), jnp.float32) for _ in range(OWN)]
                for i, tile in enumerate(tiles):
                    for k in range(CAP):
                        at = start + k
                        row = lax.shift_right_logical(at, 7)
                        lane = jnp.bitwise_and(at, EDGE - 1)
                        entry = tables[i, row, lane].astype(jnp.int32)
                        slot = lax.shift_right_arithmetic(entry, 4)
                        code = jnp.bitwise_and(jnp.maximum(entry, 0), PAIRS - 1)
                        val = tile[pl.ds(pl.multiple_of(code * EDGE, EDGE), EDGE), :]
                        for s in range(OWN):
                            want = slots[target, s] if flip else s
                            acc[s] = acc[s] + val * (slot == want).astype(jnp.float32)
                sums.append(acc)
            for s in range(OWN):
                total = sums[0][s] + flipped(sums[1][s])
                rows = pl.ds(s * EDGE, EDGE)
                if befores[j] is not None:
                    total = total + befores[j][a, rows, :]
                outs[j][a, rows, :] = total
            return carry

        lax.fori_loop(0, HIGH, dest, 0, unroll=True)


def signed(axis_size, distance):
    pairs = []
    for i in range(axis_size):
        for c in range(2):
            step = distance if c == 0 else -distance
            pairs.append((i * 2 + c, (i + step) % axis_size * 2 + c))
    return pairs


def move_x(array, distance):
    return lax.ppermute(array, ("x", "c"), signed(NX, distance))


def move_z(array, distance):
    return lax.ppermute(array, ("h", "l", "c"), signed(NZ, distance))


def gather(slots, arrays, before=()):
    n = len(arrays)
    cells = len(NEAR)
    return pl.pallas_call(
        functools.partial(gather_kernel, n, len(before) > 0),
        out_shape=[jax.ShapeDtypeStruct((HIGH, OWN * EDGE, EDGE), jnp.float32)] * cells,
        in_specs=sm(1) + vm(n + len(before)),
        out_specs=vm(cells),
        scratch_shapes=[pltpu.SMEM((n, TABLE, EDGE), jnp.float32), pltpu.SemaphoreType.DMA((n,))],
        name="gather_more" if before else "gather",
    )(slots, *[pltpu.with_memory_space_constraint(a, VMEM) for a in (*arrays, *before)])


def vm(n):
    return [pl.BlockSpec(memory_space=VMEM)] * n


def sm(n):
    return [pl.BlockSpec(memory_space=SMEM)] * n


def body(
    t2_tiles,
    cycle_ints,
    cycle_left,
    cycle_right,
    cycle_dest,
    lam_ladder,
    ladder_ints,
    ladder_mask,
    partner_slot,
    denom,
):
    f32 = jnp.float32
    payload = pl.pallas_call(
        products_kernel,
        out_shape=jax.ShapeDtypeStruct((ROWS, EDGE), f32),
        in_specs=sm(3) + vm(2),
        out_specs=pl.BlockSpec(memory_space=VMEM),
        scratch_shapes=[pltpu.SMEM((NX * NZ,), jnp.int32)],
        name="products",
    )(cycle_left[0, 0], cycle_right[0, 0], cycle_dest[0, 0], t2_tiles[0, 0], cycle_ints[0, 0])
    got_a = move_x(payload, 1)
    got_b = move_x(payload, -1)
    partial = pl.pallas_call(
        ladder_kernel,
        out_shape=jax.ShapeDtypeStruct((8, OWN * EDGE, EDGE), f32),
        in_specs=sm(1) + vm(2),
        out_specs=pl.BlockSpec(memory_space=VMEM),
        name="ladder",
    )(ladder_mask, lam_ladder, ladder_ints)
    own_slots = jnp.pad(partner_slot, ((0, 0), (0, EDGE - OWN)))
    own_slots = jnp.broadcast_to(own_slots, (NZ, 24, EDGE))
    slots = lax.all_to_all(own_slots, ("h", "l"), split_axis=0, concat_axis=0, tiled=True)
    slots = slots[:, 0, :OWN]
    got_a, got_b, partial = lax.optimization_barrier((got_a, got_b, partial))
    got_c = move_x(got_a, 1)

    near = gather(slots, (payload, got_a, got_b))
    near, partial = lax.optimization_barrier((near, partial))
    spread = lax.all_to_all(partial, ("y", "c"), split_axis=0, concat_axis=0, tiled=True)
    ladder = jnp.sum(spread, axis=0)
    n_occ = NX * NZ
    mirror = [(i, n_occ - 1 - i) for i in range(n_occ)]
    near = gather(slots, (got_c,), near)
    moved = [move_z(near[j], NEAR[j]) for j in range(3)]
    far = near[3] + moved[0] + moved[1] + moved[2]
    far, ladder = lax.optimization_barrier((far, ladder))
    other = lax.ppermute(ladder, ("x", "h", "l"), mirror)
    far = [far[0]] + [move_z(far[a], LOW * a) for a in (2, 1, 3)]
    far[3], other = lax.optimization_barrier((far[3], other))
    other = other.reshape(OWN, EDGE, EDGE)[partner_slot[0]][:, ::-1, ::-1]
    ladder = ladder + other.reshape(OWN * EDGE, EDGE)
    return (ladder + far[0] + far[1] + far[2] + far[3]) / denom


def solution(mesh):
    grid = Mesh(mesh.devices.reshape(NX, HIGH, LOW, 4, 2), ("x", "h", "l", "y", "c"))
    occ = ("x", "h", "l")
    vir = ("y", "c")
    in_specs = (
        P(occ, vir, None, None, None),
        P(occ, vir, None, None, None),
        P(occ, vir, None),
        P(occ, vir, None),
        P(occ, vir, None),
        P(occ, vir),
        P(vir, None),
        P(occ, vir),
        P(occ, None),
        P(occ, vir),
    )
    return jax.shard_map(
        body, mesh=grid, in_specs=in_specs, out_specs=P(occ, vir), check_vma=False
    )
```
